32 devices in a mesh: dp: 1, context: 16 (over z, y, x), tensor: 2 (over core).
Axes of the slice: x: 2, y: 2, z: 4, core: 2. Of those that a mesh axis runs over, the one named last changes fastest.
Arguments:
- queries: bfloat16 [1, 2048, 4096], P('dp', 'context', 'tensor'), may hold values from -30 to 30
- keys: bfloat16 [1, 2048, 256], P('dp', 'context', 'tensor'), may hold values from -4 to 4
- values: bfloat16 [1, 2048, 256], P('dp', 'context', 'tensor'), may hold values from -6 to 6
- outputs: bfloat16 [1, 2048, 4096], P('dp', 'context', 'tensor'), may hold values from -6 to 6
- grad_out: bfloat16 [1, 2048, 4096], P('dp', 'context', 'tensor'), may hold values from -24 to 24
- inputs: bfloat16 [1, 2048, 16384], P('dp', ('context', 'tensor')), may hold values from -1.5 to 1.5
- block_doc: int32 [1, 16], P('dp'), may hold values from 0 to 3, never falling along the last dimension, each value on 1 to 8 neighbouring positions
- span_slots: int32 [32], replicated, may hold values from 0 to 31, as said below
Outputs:
- grad_queries: bfloat16 [1, 2048, 4096], P('dp', 'context', 'tensor')
- grad_key_weight: float32 [16384, 256], P('context', 'tensor')
- grad_value_weight: float32 [16384, 256], P('context', 'tensor')
The draws below stay inside these ranges and needn't reach their ends.
Inputs may be any that keep to these rules, and one draw needn't show every extreme that they name: span_slots is a permutation; slots 2 d and 2 d + 1 hold two spans c and 31 - c.
All inputs are finite; a program needn't handle non-finite values.
Results may differ from the reference program's by a relative error of at most 0.0065.
Values may be sent and summed in bfloat16 or wider, within the bound.
No kernel may reach another device: no remote copies, remote signals or barrier semaphores. Data moves between devices by JAX's collectives and lax.ppermute only.
A program may use at most 64 MiB of HBM per device.

```python
import math
import jax
import jax.numpy as jnp
import numpy as np
from jax import lax

D = 16384
HEAD = 128
QGROUP = 16
DOC_BLOCK = 128
BATCH = 1
KVH = 2
QHEADS = 32
SPAN = 64
SLOTS = 32
SEQ = 2048
NBLK = 16
DOCS = 4
LONGEST = 8


def drawn_pair(key):
    first_key = jax.random.fold_in(key, 101)
    second_key = jax.random.fold_in(key, 202)
    query_draw = jnp.clip(jax.random.normal(first_key, (BATCH, SEQ, QHEADS * HEAD), jnp.float32), -4.0, 4.0)
    key_draw = jnp.clip(jax.random.normal(second_key, (BATCH, SEQ, KVH * HEAD), jnp.float32), -4.0, 4.0)
    return (query_draw, key_draw)


def draw_queries(key, part):
    return drawn_pair(key)[0].astype(jnp.bfloat16)


def draw_keys(key, part):
    return drawn_pair(key)[1].astype(jnp.bfloat16)


def draw_span_slots(key, part):
    order = jax.random.permutation(jax.random.fold_in(key, 404), SLOTS // 2).astype(jnp.int32)
    flips = jax.random.randint(jax.random.fold_in(key, 505), (SLOTS // 2,), 0, 2)
    first = jnp.where(flips == 1, SLOTS - 1 - order, order)
    second = SLOTS - 1 - first
    return jnp.stack([first, second], axis=1).reshape(SLOTS).astype(jnp.int32)


def spiked(array, key, source, target, blocks, factor):
    owner, partner = [(jnp.arange(array.shape[dim]) // (array.shape[dim] // blocks)).reshape([-1 if axis == dim else 1 for axis in range(array.ndim)]) for dim in (source, target)]
    chosen = jax.random.permutation(key, blocks)[partner]
    strong = (owner == chosen) | (owner == (partner + blocks // 2) % blocks)
    return jnp.where(strong, factor * array, array)


def shard_levels(stream_key, extent, shards, smallest, high):
    factor_of = 1.0
    for position, blocks in shards:
        draws = jax.random.uniform(jax.random.fold_in(jax.random.fold_in(stream_key, 6), position), (blocks,), jnp.float32, smallest / len(shards), high / len(shards))
        factor_of = factor_of * jnp.repeat(jnp.exp(draws), extent[position] // blocks).reshape((-1,) + (1,) * (len(extent) - 1 - position))
    return factor_of


def length_profile(amount, total, most, lean):
    loads = [(1 << 20) // math.isqrt(standing ** lean) + 1 for standing in range(2, amount + 1)]
    spare, counts = total - most - (amount - 1), [1] * (amount - 1)
    while spare > 0:
        free = [i for i in range(amount - 1) if counts[i] < most]
        mass, remaining = sum([loads[i] for i in free]), spare
        for i in free:
            addition = min(most - counts[i], max(1, remaining * loads[i] // mass), spare)
            counts[i] = counts[i] + addition
            spare = spare - addition
    return np.array([most] + counts)


def uneven(stream_key, amount, total, reach, skew):
    if amount == 2:
        one = jax.random.randint(stream_key, (), max(1, total - reach), min(reach, total - 1) + 1)
        return jnp.stack([one, total - one])
    sizes = jnp.asarray(length_profile(amount, total, reach, skew), jnp.int32)
    pairs = (amount - 1) // 2
    giver, receiver = sizes[1:1 + 2 * pairs:2], sizes[2:2 + 2 * pairs:2]
    margin = jnp.minimum(giver - 1, reach - receiver)
    moved = jax.random.randint(jax.random.fold_in(stream_key, 1), (pairs,), 0, 1 << 20) % (margin + 1)
    sizes = sizes.at[1:1 + 2 * pairs:2].set(giver - moved).at[2:2 + 2 * pairs:2].set(receiver + moved)
    return sizes[jax.random.permutation(jax.random.fold_in(stream_key, 2), amount)]


def noise(key, extent, scale, reach, pieces=(), kind=jnp.bfloat16):
    level = shard_levels(key, extent, pieces, -0.22, 0.18) if pieces else 1.0
    drawn = jax.random.normal(key, extent, jnp.float32) * scale * level
    return jnp.minimum(jnp.maximum(drawn, -reach), reach).astype(kind)


def noise_with(stream_key, shape, scale, bound, shards, heavy, held_as=jnp.bfloat16):
    drawn = scale * jax.random.normal(stream_key, shape, jnp.float32)
    if shards:
        drawn = drawn * shard_levels(stream_key, shape, shards, -0.22, 0.18)
    return jnp.clip(spiked(drawn, jax.random.fold_in(stream_key, 3), *heavy), -bound, bound).astype(held_as)


def setup_inputs(seed: int = 0) -> dict:
    seeds = jax.random.split(jax.random.key(seed), 9)
    return {
        "queries": draw_queries(jax.random.fold_in(seeds[8], 71), 0),
        "keys": draw_keys(jax.random.fold_in(seeds[8], 71), 0),
        "values": noise(seeds[2], (BATCH, SEQ, KVH * HEAD), 1.0, 6.0, ((1, 16), (2, 2))),
        "outputs": noise(seeds[3], (BATCH, SEQ, QHEADS * HEAD), 1.0, 6.0, ((1, 16), (2, 2))),
        "grad_out": noise(seeds[4], (BATCH, SEQ, QHEADS * HEAD), 4.0, 24.0, ((1, 16), (2, 2))),
        "inputs": noise_with(seeds[5], (BATCH, SEQ, D), 0.25, 1.5, ((1, 32),), (1, 2, 32, 2.75)),
        "block_doc": jax.vmap(lambda own: jnp.searchsorted(jnp.cumsum(uneven(own, DOCS, NBLK, LONGEST, 2)), jnp.arange(NBLK), side="right"))(jax.random.split(seeds[6], BATCH)).reshape((BATCH, NBLK)).astype(jnp.int32),
        "span_slots": draw_span_slots(jax.random.fold_in(seeds[8], 71), 0),
    }


def rounded(values_in):
    return lax.optimization_barrier(values_in.astype(jnp.bfloat16)).astype(jnp.float32)

def reference(queries, keys, values, outputs, grad_out, inputs, block_doc, span_slots):
    scaling = 1.0 / math.sqrt(HEAD)
    slot_index = jnp.arange(SLOTS, dtype=jnp.int32)
    inverse = lax.optimization_barrier(jnp.sum(jnp.where(span_slots[None, :] == slot_index[:, None], slot_index[None, :], 0), axis=1)).astype(jnp.int32)

    def to_positions(stored):
        return stored.reshape(stored.shape[0], SLOTS, SPAN, stored.shape[2])[:, inverse].reshape(stored.shape)

    def to_storage(ordered):
        return ordered.reshape(SLOTS, SPAN, ordered.shape[1])[span_slots].reshape(ordered.shape)
    query_order = to_positions(queries)
    key_order = to_positions(keys)
    value_order = to_positions(values)
    output_order = to_positions(outputs)
    grad_order = to_positions(grad_out)
    key_document = jnp.repeat(block_doc, DOC_BLOCK, axis=1)
    query_block = min(512, SEQ)
    positions = jnp.arange(SEQ, dtype=jnp.int32)
    width_group = QGROUP * HEAD
    batch_grads = []
    key_weight = jnp.zeros((D, KVH * HEAD), jnp.float32)
    value_weight = jnp.zeros((D, KVH * HEAD), jnp.float32)
    for batch_row in range(BATCH):
        head_grads = []
        key_parts = []
        value_parts = []
        documents = key_document[batch_row]
        for kv_head in range(KVH):
            lead = kv_head * width_group
            query_head_rows = query_order[batch_row, :, lead:lead + width_group].astype(jnp.float32).reshape(SEQ, QGROUP, HEAD)
            gradient_heads = grad_order[batch_row, :, lead:lead + width_group].astype(jnp.float32).reshape(SEQ, QGROUP, HEAD)
            output_heads = output_order[batch_row, :, lead:lead + width_group].astype(jnp.float32).reshape(SEQ, QGROUP, HEAD)
            key_rows = key_order[batch_row, :, kv_head * HEAD:(kv_head + 1) * HEAD].astype(jnp.float32)
            value_rows = value_order[batch_row, :, kv_head * HEAD:(kv_head + 1) * HEAD].astype(jnp.float32)

            def one_block(carried, block_number):
                key_grad, value_grad = carried
                first_row = block_number * query_block
                query_part = lax.dynamic_slice_in_dim(query_head_rows, first_row, query_block, 0)
                grad_part = lax.dynamic_slice_in_dim(gradient_heads, first_row, query_block, 0)
                output_part = lax.dynamic_slice_in_dim(output_heads, first_row, query_block, 0)
                query_place = first_row + jnp.arange(query_block, dtype=jnp.int32)
                query_docs = lax.dynamic_slice_in_dim(documents, first_row, query_block, 0)
                allowed = ((positions[None, :] <= query_place[:, None]) & (documents[None, :] == query_docs[:, None]))[None]
                scores = jnp.einsum('qgd,kd->gqk', query_part, key_rows) * scaling
                row_max = lax.optimization_barrier(jnp.max(jnp.where(allowed, scores, -jnp.inf), axis=2, keepdims=True))
                log_norm = row_max + jnp.log(lax.optimization_barrier(jnp.sum(jnp.where(allowed, jnp.exp(scores - row_max), 0.0), axis=2, keepdims=True)))
                attention = jnp.where(allowed, jnp.exp(scores - log_norm), 0.0)
                row_delta = jnp.transpose(lax.optimization_barrier(jnp.sum(grad_part * output_part, axis=2)))[:, :, None]
                attention_grad = jnp.einsum('qgd,kd->gqk', grad_part, value_rows)
                score_gradient = rounded(attention * (attention_grad - row_delta))
                query_grad = (jnp.einsum('gqk,kd->qgd', score_gradient, key_rows) * scaling).astype(jnp.bfloat16)
                key_grad = key_grad + jnp.einsum('gqk,qgd->kd', score_gradient, query_part) * scaling
                value_grad = value_grad + jnp.einsum('gqk,qgd->kd', rounded(attention), grad_part)
                return ((key_grad, value_grad), query_grad)
            zero_rows = jnp.zeros((SEQ, HEAD), jnp.float32)
            (key_grad, value_grad), query_grad = lax.scan(one_block, (zero_rows, zero_rows), jnp.arange(SEQ // query_block))
            head_grads.append(query_grad.reshape(SEQ, width_group))
            key_parts.append(key_grad)
            value_parts.append(value_grad)
        batch_grads.append(to_storage(jnp.concatenate(head_grads, axis=1)))
        key_low = to_storage(jnp.concatenate(key_parts, axis=1)).astype(jnp.bfloat16)
        value_lowered = to_storage(jnp.concatenate(value_parts, axis=1)).astype(jnp.bfloat16)
        key_weight = key_weight + jnp.dot(inputs[batch_row].T, key_low, preferred_element_type=jnp.float32)
        value_weight = value_weight + jnp.dot(inputs[batch_row].T, value_lowered, preferred_element_type=jnp.float32)
    return (jnp.stack(batch_grads, axis=0), key_weight, value_weight)
```

```python
import functools
import math

import jax
import jax.numpy as jnp
from jax import lax
from jax.experimental import pallas as pl
from jax.experimental.pallas import tpu as pltpu
from jax.sharding import PartitionSpec as P

NT = (((1,), (1,)), ((), ()))
NN = (((1,), (0,)), ((), ()))
TN = (((0,), (0,)), ((), ()))

LOW = 4


def dot(left, right, dims):
    return lax.dot_general(left, right, dims, preferred_element_type=jnp.float32)


def swap(value, offset, count):
    return lax.ppermute(value, "context", [(i, i ^ offset) for i in range(count)])


def attention_kernel(
    me, slots, docs, q_ref, do_ref, delta_ref, *refs, low, span_rows, block_tokens, chunk, heads, head,
):
    kv_refs, (dq_ref, *dkv_refs), scratch = refs[:low], refs[low : 2 * low + 1], refs[2 * low + 1 :]
    k_pos, v_pos, q_rows, do_rows, scores, grads, query_grad = scratch
    slot_count = slots.shape[0]
    block_count = docs.shape[0]
    total = span_rows * slot_count
    lanes = heads * span_rows
    scaling = 1.0 / math.sqrt(head)
    log2e = 1.4426950408889634
    own = me[0]

    def spans_of_pieces():
        for r in range(slot_count // 2):
            for half in range(2):
                span = slots[2 * (own ^ r) + half]
                place = pl.ds(pl.multiple_of(span * span_rows, span_rows), span_rows)
                yield r % low, pl.ds((2 * (r // low) + half) * span_rows, span_rows), place

    for piece, rows, place in spans_of_pieces():
        k_pos[place, :] = kv_refs[piece][rows, :head]
        v_pos[place, :] = kv_refs[piece][rows, head:]
    k_pos[total:, :] = jnp.zeros((chunk, head), k_pos.dtype)
    v_pos[total:, :] = jnp.zeros((chunk, head), v_pos.dtype)
    grads[...] = jnp.zeros_like(grads)

    for local in range(2):
        span = slots[2 * own + local]
        document = docs[span * span_rows // block_tokens]
        first_block = lax.fori_loop(
            0, block_count, lambda b, n: n + (docs[b] < document).astype(jnp.int32), jnp.int32(0)
        )
        first = first_block * block_tokens
        chunks = ((span + 1) * span_rows - first + chunk - 1) // chunk
        for h in range(heads):
            source = (slice(local * span_rows, (local + 1) * span_rows), slice(h * head, (h + 1) * head))
            q_rows[h * span_rows : (h + 1) * span_rows, :] = q_ref[source]
            do_rows[h * span_rows : (h + 1) * span_rows, :] = do_ref[source]

        def key_place(i):
            return pl.ds(pl.multiple_of(first + i * chunk, span_rows), chunk)

        def score_place(i):
            return pl.ds(pl.multiple_of(i * chunk, chunk), chunk)

        row_in_span = lax.broadcasted_iota(jnp.int32, (chunk, lanes), 1) % span_rows
        key_in_chunk = lax.broadcasted_iota(jnp.int32, (chunk, lanes), 0)
        ahead = key_in_chunk - row_in_span

        def raw_scores(i, largest):
            found = dot(k_pos[key_place(i), :], q_rows[...], NT)
            found = jnp.where(ahead <= span * span_rows - first - i * chunk, found, -1e30)
            scores[score_place(i), :] = found
            return jnp.maximum(largest, jnp.max(found.reshape(chunk // 8, 8, lanes), axis=0))

        largest = lax.fori_loop(0, chunks, raw_scores, jnp.full((8, lanes), -1e30, jnp.float32))
        largest = jnp.max(largest, axis=0, keepdims=True)

        def weigh(i, total_weight):
            weight = jnp.exp2((scores[score_place(i), :] - largest) * (scaling * log2e))
            scores[score_place(i), :] = weight
            return total_weight + jnp.sum(weight.reshape(chunk // 8, 8, lanes), axis=0)

        weight_sum = lax.fori_loop(0, chunks, weigh, jnp.zeros((8, lanes), jnp.float32))
        inverse = 1.0 / jnp.sum(weight_sum, axis=0, keepdims=True)
        delta = delta_ref[local]

        query_grad[...] = jnp.zeros_like(query_grad)

        def gradients(i, carry):
            attention = scores[score_place(i), :] * inverse
            attention_grad = dot(v_pos[key_place(i), :], do_rows[...], NT)
            score_grad = (attention * (attention_grad - delta)).astype(jnp.bfloat16)
            keys = k_pos[key_place(i), :]
            grads[key_place(i), :head] += dot(score_grad, q_rows[...], NN)
            grads[key_place(i), head:] += dot(attention.astype(jnp.bfloat16), do_rows[...], NN)
            query_grad[...] += dot(keys, score_grad, TN)
            return carry

        lax.fori_loop(0, chunks, gradients, 0)
        turned = (query_grad[...] * scaling).T.astype(dq_ref.dtype)
        for h in range(heads):
            dq_ref[local * span_rows : (local + 1) * span_rows, h * head : (h + 1) * head] = turned[
                h * span_rows : (h + 1) * span_rows, :
            ]

    for piece, rows, place in spans_of_pieces():
        dkv_refs[piece][rows, :head] = (grads[place, :head] * scaling).astype(jnp.bfloat16)
        dkv_refs[piece][rows, head:] = grads[place, head:].astype(jnp.bfloat16)


def attention_grads(me, slots, docs, queries, grad_out, delta, key_values, head, block_tokens):
    rows, width = queries.shape
    low = len(key_values)
    total = low * key_values[0].shape[0]
    heads = width // head
    span_rows = rows // 2
    chunk = min(256, total)
    vmem = pl.BlockSpec(memory_space=pltpu.VMEM)
    smem = pl.BlockSpec(memory_space=pltpu.SMEM)
    lanes = heads * span_rows
    body = functools.partial(
        attention_kernel, low=low, span_rows=span_rows, block_tokens=block_tokens, chunk=chunk, heads=heads, head=head
    )
    return pl.pallas_call(
        body,
        out_shape=(
            jax.ShapeDtypeStruct((rows, width), jnp.bfloat16),
            *(jax.ShapeDtypeStruct((total // low, 2 * head), jnp.bfloat16) for _ in range(low)),
        ),
        in_specs=[smem, smem, smem, vmem, vmem, vmem] + [vmem] * low,
        out_specs=(vmem,) * (low + 1),
        scratch_shapes=[
            pltpu.VMEM((total + chunk, head), jnp.bfloat16),
            pltpu.VMEM((total + chunk, head), jnp.bfloat16),
            pltpu.VMEM((lanes, head), jnp.bfloat16),
            pltpu.VMEM((lanes, head), jnp.bfloat16),
            pltpu.VMEM((total + chunk, lanes), jnp.float32),
            pltpu.VMEM((total + chunk, 2 * head), jnp.float32),
            pltpu.VMEM((head, lanes), jnp.float32),
        ],
        compiler_params=pltpu.CompilerParams(vmem_limit_bytes=48 << 20),
        name="attention_grads",
    )(me, slots, docs, queries, grad_out, delta, *key_values)


def turned_columns(me, halves, rows, column_count):
    count = halves[0].shape[0]
    spec = pl.BlockSpec((1, rows, column_count), lambda r, me: (me[0] ^ r, 0, 0))
    tensor_count = len(halves)

    def body(me, *refs):
        both = jnp.concatenate([ref[0] for ref in refs[:-1]], axis=0)
        refs[-1][...] = both.T

    return pl.pallas_call(
        body,
        out_shape=jax.ShapeDtypeStruct((column_count, count * tensor_count * rows), jnp.bfloat16),
        grid_spec=pltpu.PrefetchScalarGridSpec(
            num_scalar_prefetch=1,
            grid=(count,),
            in_specs=[spec] * tensor_count,
            out_specs=pl.BlockSpec((column_count, tensor_count * rows), lambda r, me: (0, r)),
        ),
        name="turned_columns",
    )(me, *halves)


def on_device(queries, keys, values, outputs, grad_out, inputs, block_doc, span_slots):
    batch_count, row_count, query_width = queries.shape
    head = keys.shape[2]
    heads = query_width // head
    span_rows = row_count // 2
    total = span_rows * span_slots.shape[0]
    block_tokens = total // block_doc.shape[1]
    count = total // row_count
    low = min(LOW, count)
    high = count // low
    token_rows = inputs.shape[1]
    tensor_count = row_count // token_rows
    column_count = inputs.shape[2] // count
    me = lax.axis_index("context").astype(jnp.int32).reshape(1)

    sent = inputs.reshape(batch_count, token_rows, count, column_count)
    sent = jnp.moveaxis(sent, 2, 0).reshape(count, batch_count * token_rows, column_count)
    mine = lax.all_to_all(sent, "context", split_axis=0, concat_axis=0, tiled=True)
    tensor_index = lax.axis_index("tensor")
    if tensor_count == 2:
        other = lax.ppermute(mine, "tensor", [(0, 1), (1, 0)])
        halves = [jnp.where(tensor_index == 0, mine, other), jnp.where(tensor_index == 0, other, mine)]
    else:
        every = lax.all_gather(mine, "tensor", axis=0)
        halves = [every[t] for t in range(tensor_count)]

    own = jnp.concatenate([keys, values], axis=2)
    column = jnp.concatenate([own] + [swap(own, k * low, count) for k in range(1, high)], axis=1)
    key_values = [column] + [swap(column, k, count) for k in range(1, low)]

    delta = jnp.einsum(
        "bqgd,bqgd->bgq",
        grad_out.reshape(batch_count, row_count, heads, head),
        outputs.reshape(batch_count, row_count, heads, head),
        preferred_element_type=jnp.float32,
    )
    delta = delta.reshape(batch_count, heads, 2, span_rows).swapaxes(1, 2).reshape(batch_count, 2, 1, heads * span_rows)

    query_grads, weight_grads = [], []
    for b in range(batch_count):
        query_grad, *partials = attention_grads(
            me, span_slots, block_doc[b], queries[b], grad_out[b], delta[b], [kv[b] for kv in key_values], head, block_tokens
        )
        query_grads.append(query_grad)
        arrived = [partials[0]] + [swap(partials[k], k, count) for k in range(1, low)]
        sums = sum(p.astype(jnp.float32) for p in arrived)
        pieces = [sums[k * row_count : (k + 1) * row_count] for k in range(high)]
        arrived = [pieces[0]] + [swap(pieces[k].astype(jnp.bfloat16), k * low, count) for k in range(1, high)]
        own_grads = sum(p.astype(jnp.float32) for p in arrived).astype(jnp.bfloat16)
        column = jnp.concatenate([own_grads] + [swap(own_grads, k * low, count) for k in range(1, high)], axis=0)
        columns = [column] + [swap(column, k, count) for k in range(1, low)]
        all_grads = jnp.stack([c.reshape(high, row_count, 2 * head) for c in columns], axis=1).reshape(total, 2 * head)
        own_halves = [h[:, b * token_rows : (b + 1) * token_rows] for h in halves]
        turned = turned_columns(me, own_halves, token_rows, column_count)
        weight_grads.append(dot(turned, all_grads, NN))
    summed = lax.psum(sum(weight_grads), "dp")
    return jnp.stack(query_grads), summed[:, :head], summed[:, head:]


def solution(mesh):
    in_specs = (
        P("dp", "context", "tensor"),
        P("dp", "context", "tensor"),
        P("dp", "context", "tensor"),
        P("dp", "context", "tensor"),
        P("dp", "context", "tensor"),
        P("dp", ("context", "tensor"), None),
        P("dp", None),
        P(),
    )
    out_specs = (P("dp", "context", "tensor"), P("context", "tensor"), P("context", "tensor"))
    return jax.shard_map(on_device, mesh=mesh, in_specs=in_specs, out_specs=out_specs, check_vma=False)
```

```python
import functools
import math

import jax
import jax.numpy as jnp
from jax import lax
from jax.experimental import pallas as pl
from jax.experimental.pallas import tpu as pltpu
from jax.sharding import PartitionSpec as P

NT = (((1,), (1,)), ((), ()))
NN = (((1,), (0,)), ((), ()))
TN = (((0,), (0,)), ((), ()))

LOW = 4


def dot(left, right, dims):
    return lax.dot_general(left, right, dims, preferred_element_type=jnp.float32)


def swap(value, offset, count):
    return lax.ppermute(value, "context", [(i, i ^ offset) for i in range(count)])


def attention_kernel(
    me, slots, docs, q_ref, do_ref, delta_ref, *refs, low, span_rows, block_tokens, chunk, heads, head,
):
    kv_refs, (dq_ref, *dkv_refs), scratch = refs[:low], refs[low : 2 * low + 1], refs[2 * low + 1 :]
    k_pos, v_pos, q_rows, do_rows, scores, grads, query_grad = scratch
    slot_count = slots.shape[0]
    block_count = docs.shape[0]
    total = span_rows * slot_count
    lanes = heads * span_rows
    scaling = 1.0 / math.sqrt(head)
    log2e = 1.4426950408889634
    own = me[0]

    def spans_of_pieces():
        for r in range(slot_count // 2):
            for half in range(2):
                span = slots[2 * (own ^ r) + half]
                place = pl.ds(pl.multiple_of(span * span_rows, span_rows), span_rows)
                yield r % low, pl.ds((2 * (r // low) + half) * span_rows, span_rows), place

    for piece, rows, place in spans_of_pieces():
        k_pos[place, :] = kv_refs[piece][rows, :head]
        v_pos[place, :] = kv_refs[piece][rows, head:]
    k_pos[total:, :] = jnp.zeros((chunk, head), k_pos.dtype)
    v_pos[total:, :] = jnp.zeros((chunk, head), v_pos.dtype)
    grads[...] = jnp.zeros_like(grads)

    for local in range(2):
        span = slots[2 * own + local]
        document = docs[span * span_rows // block_tokens]
        first_block = lax.fori_loop(
            0, block_count, lambda b, n: n + (docs[b] < document).astype(jnp.int32), jnp.int32(0)
        )
        first = first_block * block_tokens
        chunks = ((span + 1) * span_rows - first + chunk - 1) // chunk
        for h in range(heads):
            source = (slice(local * span_rows, (local + 1) * span_rows), slice(h * head, (h + 1) * head))
            q_rows[h * span_rows : (h + 1) * span_rows, :] = q_ref[source]
            do_rows[h * span_rows : (h + 1) * span_rows, :] = do_ref[source]

        def key_place(i):
            return pl.ds(pl.multiple_of(first + i * chunk, span_rows), chunk)

        def score_place(i):
            return pl.ds(pl.multiple_of(i * chunk, chunk), chunk)

        row_in_span = lax.broadcasted_iota(jnp.int32, (chunk, lanes), 1) % span_rows
        key_in_chunk = lax.broadcasted_iota(jnp.int32, (chunk, lanes), 0)
        ahead = key_in_chunk - row_in_span

        def raw_scores(i, largest):
            found = dot(k_pos[key_place(i), :], q_rows[...], NT)
            found = jnp.where(ahead <= span * span_rows - first - i * chunk, found, -1e30)
            scores[score_place(i), :] = found
            return jnp.maximum(largest, jnp.max(found.reshape(chunk // 8, 8, lanes), axis=0))

        largest = lax.fori_loop(0, chunks, raw_scores, jnp.full((8, lanes), -1e30, jnp.float32))
        largest = jnp.max(largest, axis=0, keepdims=True)

        def weigh(i, total_weight):
            weight = jnp.exp2((scores[score_place(i), :] - largest) * (scaling * log2e))
            scores[score_place(i), :] = weight
            return total_weight + jnp.sum(weight.reshape(chunk // 8, 8, lanes), axis=0)

        weight_sum = lax.fori_loop(0, chunks, weigh, jnp.zeros((8, lanes), jnp.float32))
        inverse = 1.0 / jnp.sum(weight_sum, axis=0, keepdims=True)
        delta = delta_ref[local]

        query_grad[...] = jnp.zeros_like(query_grad)

        def gradients(i, carry):
            attention = scores[score_place(i), :] * inverse
            attention_grad = dot(v_pos[key_place(i), :], do_rows[...], NT)
            score_grad = (attention * (attention_grad - delta)).astype(jnp.bfloat16)
            keys = k_pos[key_place(i), :]
            grads[key_place(i), :head] += dot(score_grad, q_rows[...], NN)
            grads[key_place(i), head:] += dot(attention.astype(jnp.bfloat16), do_rows[...], NN)
            query_grad[...] += dot(keys, score_grad, TN)
            return carry

        lax.fori_loop(0, chunks, gradients, 0)
        turned = (query_grad[...] * scaling).T.astype(dq_ref.dtype)
        for h in range(heads):
            dq_ref[local * span_rows : (local + 1) * span_rows, h * head : (h + 1) * head] = turned[
                h * span_rows : (h + 1) * span_rows, :
            ]

    for piece, rows, place in spans_of_pieces():
        dkv_refs[piece][rows, :head] = (grads[place, :head] * scaling).astype(jnp.bfloat16)
        dkv_refs[piece][rows, head:] = grads[place, head:].astype(jnp.bfloat16)


def attention_grads(me, slots, docs, queries, grad_out, delta, key_values, head, block_tokens):
    rows, width = queries.shape
    low = len(key_values)
    total = low * key_values[0].shape[0]
    heads = width // head
    span_rows = rows // 2
    chunk = min(256, total)
    vmem = pl.BlockSpec(memory_space=pltpu.VMEM)
    smem = pl.BlockSpec(memory_space=pltpu.SMEM)
    lanes = heads * span_rows
    body = functools.partial(
        attention_kernel, low=low, span_rows=span_rows, block_tokens=block_tokens, chunk=chunk, heads=heads, head=head
    )
    return pl.pallas_call(
        body,
        out_shape=(
            jax.ShapeDtypeStruct((rows, width), jnp.bfloat16),
            *(jax.ShapeDtypeStruct((total // low, 2 * head), jnp.bfloat16) for _ in range(low)),
        ),
        in_specs=[smem, smem, smem, vmem, vmem, vmem] + [vmem] * low,
        out_specs=(vmem,) * (low + 1),
        scratch_shapes=[
            pltpu.VMEM((total + chunk, head), jnp.bfloat16),
            pltpu.VMEM((total + chunk, head), jnp.bfloat16),
            pltpu.VMEM((lanes, head), jnp.bfloat16),
            pltpu.VMEM((lanes, head), jnp.bfloat16),
            pltpu.VMEM((total + chunk, lanes), jnp.float32),
            pltpu.VMEM((total + chunk, 2 * head), jnp.float32),
            pltpu.VMEM((head, lanes), jnp.float32),
        ],
        compiler_params=pltpu.CompilerParams(vmem_limit_bytes=48 << 20),
        name="attention_grads",
    )(me, slots, docs, queries, grad_out, delta, *key_values)


def weight_kernel(place, *refs, low, parts, rows, head):
    grad_refs, column_refs, (key_ref, value_ref, sums) = refs[:low], refs[low : low + parts], refs[low + parts :]
    step = pl.program_id(0)
    own_high, own_part = place[0] // low, place[1]
    high = column_refs[0].shape[0]
    tokens = jnp.concatenate([ref[h, 0] for ref in column_refs for h in range(high)], axis=0)

    for digit in range(low):

        @pl.when(step == digit)
        def _():
            starts = [((h ^ own_high) * parts + (part ^ own_part)) * rows for part in range(parts) for h in range(high)]
            grads = jnp.concatenate([grad_refs[digit][pl.ds(pl.multiple_of(s, rows), rows), :] for s in starts], axis=0)
            found = dot(grads, tokens, TN)
            sums[...] = found if digit == 0 else sums[...] + found

    @pl.when(step == low - 1)
    def _():
        key_ref[...] = sums[:head, :].T
        value_ref[...] = sums[head:, :].T


def weight_grads(place, columns, grads, head):
    count, rows, width = columns[0].shape
    low, parts = len(grads), len(columns)
    spec = pl.BlockSpec((count // low, 1, rows, width), lambda i, place: (0, (place[0] % low) ^ i, 0, 0))
    whole = pl.BlockSpec(grads[0].shape, lambda i, place: (0, 0))
    out = pl.BlockSpec((width, head), lambda i, place: (0, 0))
    return pl.pallas_call(
        functools.partial(weight_kernel, low=low, parts=parts, rows=rows, head=head),
        out_shape=(jax.ShapeDtypeStruct((width, head), jnp.float32),) * 2,
        grid_spec=pltpu.PrefetchScalarGridSpec(
            num_scalar_prefetch=1,
            grid=(low,),
            in_specs=[whole] * low + [spec] * parts,
            out_specs=(out, out),
            scratch_shapes=[pltpu.VMEM((2 * head, width), jnp.float32)],
        ),
        compiler_params=pltpu.CompilerParams(vmem_limit_bytes=32 << 20),
        name="weight_grads",
    )(place, *grads, *(c.reshape(count // low, low, rows, width) for c in columns))


def on_device(queries, keys, values, outputs, grad_out, inputs, block_doc, span_slots):
    batch_count, row_count, query_width = queries.shape
    head = keys.shape[2]
    heads = query_width // head
    span_rows = row_count // 2
    total = span_rows * span_slots.shape[0]
    block_tokens = total // block_doc.shape[1]
    count = total // row_count
    low = min(LOW, count)
    high = count // low
    token_rows = inputs.shape[1]
    tensor_count = row_count // token_rows
    column_count = inputs.shape[2] // count
    me = lax.axis_index("context").astype(jnp.int32).reshape(1)

    own = jnp.concatenate([keys, values], axis=2)
    column = jnp.concatenate([own] + [swap(own, k * low, count) for k in range(1, high)], axis=1)
    key_values = [column] + [swap(column, k, count) for k in range(1, low)]

    sent = inputs.reshape(batch_count, token_rows, count, column_count)
    sent = jnp.moveaxis(sent, 2, 0).reshape(count, batch_count * token_rows, column_count)
    sent, _ = lax.optimization_barrier((sent, column))
    mine = lax.all_to_all(sent, "context", split_axis=0, concat_axis=0, tiled=True)

    delta = jnp.einsum(
        "bqgd,bqgd->bgq",
        grad_out.reshape(batch_count, row_count, heads, head),
        outputs.reshape(batch_count, row_count, heads, head),
        preferred_element_type=jnp.float32,
    )
    delta = delta.reshape(batch_count, heads, 2, span_rows).swapaxes(1, 2).reshape(batch_count, 2, 1, heads * span_rows)

    place = jnp.concatenate([me, lax.axis_index("tensor").astype(jnp.int32).reshape(1)])
    query_grads, key_sums, value_sums = [], 0.0, 0.0
    for b in range(batch_count):
        query_grad, *partials = attention_grads(
            me, span_slots, block_doc[b], queries[b], grad_out[b], delta[b], [kv[b] for kv in key_values], head, block_tokens
        )
        query_grads.append(query_grad)
        arrived = [partials[0]] + [swap(partials[k], k, count) for k in range(1, low)]
        sums = sum(p.astype(jnp.float32) for p in arrived)
        pieces = [sums[k * row_count : (k + 1) * row_count] for k in range(high)]
        arrived = [pieces[0]] + [swap(pieces[k].astype(jnp.bfloat16), k * low, count) for k in range(1, high)]
        own_grads = sum(p.astype(jnp.float32) for p in arrived).astype(jnp.bfloat16)
        column = jnp.concatenate([own_grads] + [swap(own_grads, k * low, count) for k in range(1, high)], axis=0)
        columns = [column] + [swap(column, k, count) for k in range(1, low)]
        late, _ = lax.optimization_barrier((mine[:, b * token_rows : (b + 1) * token_rows], own_grads))
        parts = [late] + [
            lax.ppermute(late, "tensor", [(i, i ^ k) for i in range(tensor_count)]) for k in range(1, tensor_count)
        ]
        key_part, value_part = weight_grads(place, parts, columns, head)
        key_sums, value_sums = key_sums + key_part, value_sums + value_part
    return jnp.stack(query_grads), lax.psum(key_sums, "dp"), lax.psum(value_sums, "dp")


def solution(mesh):
    in_specs = (
        P("dp", "context", "tensor"),
        P("dp", "context", "tensor"),
        P("dp", "context", "tensor"),
        P("dp", "context", "tensor"),
        P("dp", "context", "tensor"),
        P("dp", ("context", "tensor"), None),
        P("dp", None),
        P(),
    )
    out_specs = (P("dp", "context", "tensor"), P("context", "tensor"), P("context", "tensor"))
    return jax.shard_map(on_device, mesh=mesh, in_specs=in_specs, out_specs=out_specs, check_vma=False)
```

```python
import functools
import math

import jax
import jax.numpy as jnp
from jax import lax
from jax.experimental import pallas as pl
from jax.experimental.pallas import tpu as pltpu
from jax.sharding import PartitionSpec as P

NT = (((1,), (1,)), ((), ()))
NN = (((1,), (0,)), ((), ()))
TN = (((0,), (0,)), ((), ()))

LOW = 4


def dot(left, right, dims):
    return lax.dot_general(left, right, dims, preferred_element_type=jnp.float32)


def swap(value, offset, count):
    return lax.ppermute(value, "context", [(i, i ^ offset) for i in range(count)])


def attention_kernel(
    me, slots, docs, q_ref, do_ref, delta_ref, *refs, low, span_rows, block_tokens, chunk, heads, head,
):
    kv_refs, (dq_ref, *dkv_refs), scratch = refs[:low], refs[low : 2 * low + 1], refs[2 * low + 1 :]
    k_pos, v_pos, q_rows, do_rows, scores, grads, query_grad = scratch
    slot_count = slots.shape[0]
    block_count = docs.shape[0]
    total = span_rows * slot_count
    lanes = heads * span_rows
    scaling = 1.0 / math.sqrt(head)
    log2e = 1.4426950408889634
    own = me[0]

    def spans_of_pieces():
        for r in range(slot_count // 2):
            for half in range(2):
                span = slots[2 * (own ^ r) + half]
                place = pl.ds(pl.multiple_of(span * span_rows, span_rows), span_rows)
                yield r % low, pl.ds((2 * (r // low) + half) * span_rows, span_rows), place

    for piece, rows, place in spans_of_pieces():
        k_pos[place, :] = kv_refs[piece][rows, :head]
        v_pos[place, :] = kv_refs[piece][rows, head:]
    k_pos[total:, :] = jnp.zeros((chunk, head), k_pos.dtype)
    v_pos[total:, :] = jnp.zeros((chunk, head), v_pos.dtype)
    grads[...] = jnp.zeros_like(grads)

    for local in range(2):
        span = slots[2 * own + local]
        document = docs[span * span_rows // block_tokens]
        first_block = lax.fori_loop(
            0, block_count, lambda b, n: n + (docs[b] < document).astype(jnp.int32), jnp.int32(0)
        )
        first = first_block * block_tokens
        chunks = ((span + 1) * span_rows - first + chunk - 1) // chunk
        for h in range(heads):
            source = (slice(local * span_rows, (local + 1) * span_rows), slice(h * head, (h + 1) * head))
            q_rows[h * span_rows : (h + 1) * span_rows, :] = q_ref[source]
            do_rows[h * span_rows : (h + 1) * span_rows, :] = do_ref[source]

        def key_place(i):
            return pl.ds(pl.multiple_of(first + i * chunk, span_rows), chunk)

        def score_place(i):
            return pl.ds(pl.multiple_of(i * chunk, chunk), chunk)

        row_in_span = lax.broadcasted_iota(jnp.int32, (chunk, lanes), 1) % span_rows
        key_in_chunk = lax.broadcasted_iota(jnp.int32, (chunk, lanes), 0)
        ahead = key_in_chunk - row_in_span

        def raw_scores(i, largest):
            found = dot(k_pos[key_place(i), :], q_rows[...], NT)
            found = jnp.where(ahead <= span * span_rows - first - i * chunk, found, -1e30)
            scores[score_place(i), :] = found
            return jnp.maximum(largest, jnp.max(found.reshape(chunk // 8, 8, lanes), axis=0))

        largest = lax.fori_loop(0, chunks, raw_scores, jnp.full((8, lanes), -1e30, jnp.float32))
        largest = jnp.max(largest, axis=0, keepdims=True)

        def weigh(i, total_weight):
            weight = jnp.exp2((scores[score_place(i), :] - largest) * (scaling * log2e))
            scores[score_place(i), :] = weight
            return total_weight + jnp.sum(weight.reshape(chunk // 8, 8, lanes), axis=0)

        weight_sum = lax.fori_loop(0, chunks, weigh, jnp.zeros((8, lanes), jnp.float32))
        inverse = 1.0 / jnp.sum(weight_sum, axis=0, keepdims=True)
        delta = delta_ref[local]

        query_grad[...] = jnp.zeros_like(query_grad)

        def gradients(i, carry):
            attention = scores[score_place(i), :] * inverse
            attention_grad = dot(v_pos[key_place(i), :], do_rows[...], NT)
            score_grad = (attention * (attention_grad - delta)).astype(jnp.bfloat16)
            keys = k_pos[key_place(i), :]
            grads[key_place(i), :head] += dot(score_grad, q_rows[...], NN)
            grads[key_place(i), head:] += dot(attention.astype(jnp.bfloat16), do_rows[...], NN)
            query_grad[...] += dot(keys, score_grad, TN)
            return carry

        lax.fori_loop(0, chunks, gradients, 0)
        turned = (query_grad[...] * scaling).T.astype(dq_ref.dtype)
        for h in range(heads):
            dq_ref[local * span_rows : (local + 1) * span_rows, h * head : (h + 1) * head] = turned[
                h * span_rows : (h + 1) * span_rows, :
            ]

    for piece, rows, place in spans_of_pieces():
        dkv_refs[piece][rows, :head] = (grads[place, :head] * scaling).astype(jnp.bfloat16)
        dkv_refs[piece][rows, head:] = grads[place, head:].astype(jnp.bfloat16)


def attention_grads(me, slots, docs, queries, grad_out, delta, key_values, head, block_tokens):
    rows, width = queries.shape
    low = len(key_values)
    total = low * key_values[0].shape[0]
    heads = width // head
    span_rows = rows // 2
    chunk = min(256, total)
    vmem = pl.BlockSpec(memory_space=pltpu.VMEM)
    smem = pl.BlockSpec(memory_space=pltpu.SMEM)
    lanes = heads * span_rows
    body = functools.partial(
        attention_kernel, low=low, span_rows=span_rows, block_tokens=block_tokens, chunk=chunk, heads=heads, head=head
    )
    return pl.pallas_call(
        body,
        out_shape=(
            jax.ShapeDtypeStruct((rows, width), jnp.bfloat16),
            *(jax.ShapeDtypeStruct((total // low, 2 * head), jnp.bfloat16) for _ in range(low)),
        ),
        in_specs=[smem, smem, smem, vmem, vmem, vmem] + [vmem] * low,
        out_specs=(vmem,) * (low + 1),
        scratch_shapes=[
            pltpu.VMEM((total + chunk, head), jnp.bfloat16),
            pltpu.VMEM((total + chunk, head), jnp.bfloat16),
            pltpu.VMEM((lanes, head), jnp.bfloat16),
            pltpu.VMEM((lanes, head), jnp.bfloat16),
            pltpu.VMEM((total + chunk, lanes), jnp.float32),
            pltpu.VMEM((total + chunk, 2 * head), jnp.float32),
            pltpu.VMEM((head, lanes), jnp.float32),
        ],
        compiler_params=pltpu.CompilerParams(vmem_limit_bytes=48 << 20),
        name="attention_grads",
    )(me, slots, docs, queries, grad_out, delta, *key_values)


def weight_kernel(place, grad_ref, *refs, low, parts, rows, digit, head):
    column_refs, refs = refs[:parts], refs[parts:]
    own_high, own_part = place[0] // low, place[1]
    high = column_refs[0].shape[0]
    tokens = jnp.concatenate([ref[...].reshape(high * rows, ref.shape[-1]) for ref in column_refs], axis=0)
    starts = [((h ^ own_high) * parts + (part ^ own_part)) * rows for part in range(parts) for h in range(high)]
    grads = jnp.concatenate([grad_ref[pl.ds(pl.multiple_of(s, rows), rows), :] for s in starts], axis=0)
    found = dot(grads, tokens, TN)
    if digit:
        found = refs[0][...] + found
    if digit == low - 1:
        refs[-2][...] = found[:head, :].T
        refs[-1][...] = found[head:, :].T
    else:
        refs[-1][...] = found


def weight_step(place, digit, low, columns, grads, sums, head):
    count, rows, width = columns[0].shape
    parts = len(columns)
    spec = pl.BlockSpec((count // low, 1, rows, width), lambda i, place: (0, (place[0] % low) ^ digit, 0, 0))
    shapes = ((width, head),) * 2 if digit == low - 1 else ((2 * head, width),)
    before = [sums] if digit else []
    return pl.pallas_call(
        functools.partial(weight_kernel, low=low, parts=parts, rows=rows, digit=digit, head=head),
        out_shape=tuple(jax.ShapeDtypeStruct(s, jnp.float32) for s in shapes),
        grid_spec=pltpu.PrefetchScalarGridSpec(
            num_scalar_prefetch=1,
            grid=(1,),
            in_specs=[pl.BlockSpec(grads.shape, lambda i, place: (0, 0))]
            + [spec] * parts
            + [pl.BlockSpec((2 * head, width), lambda i, place: (0, 0))] * len(before),
            out_specs=tuple(pl.BlockSpec(s, lambda i, place: (0, 0)) for s in shapes),
        ),
        compiler_params=pltpu.CompilerParams(vmem_limit_bytes=32 << 20),
        name="weight_step",
    )(place, grads, *(c.reshape(count // low, low, rows, width) for c in columns), *before)


def after(value, *others):
    return lax.optimization_barrier((value, *others))[0]


def on_device(queries, keys, values, outputs, grad_out, inputs, block_doc, span_slots):
    batch_count, row_count, query_width = queries.shape
    head = keys.shape[2]
    heads = query_width // head
    span_rows = row_count // 2
    total = span_rows * span_slots.shape[0]
    block_tokens = total // block_doc.shape[1]
    count = total // row_count
    low = min(LOW, count)
    high = count // low
    token_rows = inputs.shape[1]
    tensor_count = row_count // token_rows
    column_count = inputs.shape[2] // count
    me = lax.axis_index("context").astype(jnp.int32).reshape(1)

    own = jnp.concatenate([keys, values], axis=2)
    by_high = [own] + [swap(own, k * low, count) for k in range(1, high)]
    column = jnp.concatenate(by_high, axis=1)
    key_values = [column] + [swap(column, k, count) for k in range(1, low)]

    sent = inputs.reshape(batch_count, token_rows, count, column_count)
    sent = jnp.moveaxis(sent, 2, 0).reshape(count, batch_count * token_rows, column_count)
    sent = after(sent, column)
    mine = lax.all_to_all(sent, "context", split_axis=0, concat_axis=0, tiled=True)

    delta = jnp.einsum(
        "bqgd,bqgd->bgq",
        grad_out.reshape(batch_count, row_count, heads, head),
        outputs.reshape(batch_count, row_count, heads, head),
        preferred_element_type=jnp.float32,
    )
    delta = delta.reshape(batch_count, heads, 2, span_rows).swapaxes(1, 2).reshape(batch_count, 2, 1, heads * span_rows)

    place = jnp.concatenate([me, lax.axis_index("tensor").astype(jnp.int32).reshape(1)])
    query_grads, key_sums, value_sums = [], 0.0, 0.0
    for b in range(batch_count):
        query_grad, *partials = attention_grads(
            me, span_slots, block_doc[b], queries[b], grad_out[b], delta[b], [kv[b] for kv in key_values], head, block_tokens
        )
        query_grads.append(query_grad)
        arrived = [partials[0]] + [swap(partials[k], k, count) for k in range(1, low)]
        sums = sum(p.astype(jnp.float32) for p in arrived)
        pieces = [sums[k * row_count : (k + 1) * row_count] for k in range(high)]
        arrived = [pieces[0]] + [swap(pieces[k].astype(jnp.bfloat16), k * low, count) for k in range(1, high)]
        own_grads = sum(p.astype(jnp.float32) for p in arrived).astype(jnp.bfloat16)
        column = jnp.concatenate([own_grads] + [swap(own_grads, k * low, count) for k in range(1, high)], axis=0)
        columns = [column] + [swap(column, k, count) for k in range(1, low)]
        late = after(mine[:, b * token_rows : (b + 1) * token_rows], own_grads)
        parts = [late] + [
            lax.ppermute(late, "tensor", [(i, i ^ k) for i in range(tensor_count)]) for k in range(1, tensor_count)
        ]
        found = [None]
        for k in range(low):
            found = weight_step(place, k, low, parts, columns[k], found[0], head)
        key_sums, value_sums = key_sums + found[0], value_sums + found[1]
    return jnp.stack(query_grads), lax.psum(key_sums, "dp"), lax.psum(value_sums, "dp")


def solution(mesh):
    in_specs = (
        P("dp", "context", "tensor"),
        P("dp", "context", "tensor"),
        P("dp", "context", "tensor"),
        P("dp", "context", "tensor"),
        P("dp", "context", "tensor"),
        P("dp", ("context", "tensor"), None),
        P("dp", None),
        P(),
    )
    out_specs = (P("dp", "context", "tensor"), P("context", "tensor"), P("context", "tensor"))
    return jax.shard_map(on_device, mesh=mesh, in_specs=in_specs, out_specs=out_specs, check_vma=False)
```

```python
import functools
import math

import jax
import jax.numpy as jnp
from jax import lax
from jax.experimental import pallas as pl
from jax.experimental.pallas import tpu as pltpu
from jax.sharding import PartitionSpec as P

NT = (((1,), (1,)), ((), ()))
NN = (((1,), (0,)), ((), ()))
TN = (((0,), (0,)), ((), ()))

LOW = 4


def dot(left, right, dims):
    return lax.dot_general(left, right, dims, preferred_element_type=jnp.float32)


def swap(value, offset, count):
    return lax.ppermute(value, "context", [(i, i ^ offset) for i in range(count)])


def attention_kernel(
    me, slots, docs, q_ref, do_ref, delta_ref, *refs, low, span_rows, block_tokens, chunk, heads, head,
):
    kv_refs, (dq_ref, *dkv_refs), scratch = refs[:low], refs[low : 2 * low + 1], refs[2 * low + 1 :]
    k_pos, v_pos, q_rows, do_rows, scores, grads, query_grad = scratch
    slot_count = slots.shape[0]
    block_count = docs.shape[0]
    total = span_rows * slot_count
    lanes = heads * span_rows
    scaling = 1.0 / math.sqrt(head)
    log2e = 1.4426950408889634
    own = me[0]

    def spans_of_pieces():
        for r in range(slot_count // 2):
            for half in range(2):
                span = slots[2 * (own ^ r) + half]
                place = pl.ds(pl.multiple_of(span * span_rows, span_rows), span_rows)
                yield r % low, pl.ds((2 * (r // low) + half) * span_rows, span_rows), place

    for piece, rows, place in spans_of_pieces():
        k_pos[place, :] = kv_refs[piece][rows, :head]
        v_pos[place, :] = kv_refs[piece][rows, head:]
    k_pos[total:, :] = jnp.zeros((chunk, head), k_pos.dtype)
    v_pos[total:, :] = jnp.zeros((chunk, head), v_pos.dtype)
    grads[...] = jnp.zeros_like(grads)

    for local in range(2):
        span = slots[2 * own + local]
        document = docs[span * span_rows // block_tokens]
        first_block = lax.fori_loop(
            0, block_count, lambda b, n: n + (docs[b] < document).astype(jnp.int32), jnp.int32(0)
        )
        first = first_block * block_tokens
        chunks = ((span + 1) * span_rows - first + chunk - 1) // chunk
        for h in range(heads):
            source = (slice(local * span_rows, (local + 1) * span_rows), slice(h * head, (h + 1) * head))
            q_rows[h * span_rows : (h + 1) * span_rows, :] = q_ref[source]
            do_rows[h * span_rows : (h + 1) * span_rows, :] = do_ref[source]

        def key_place(i):
            return pl.ds(pl.multiple_of(first + i * chunk, span_rows), chunk)

        def score_place(i):
            return pl.ds(pl.multiple_of(i * chunk, chunk), chunk)

        row_in_span = lax.broadcasted_iota(jnp.int32, (chunk, lanes), 1) % span_rows
        key_in_chunk = lax.broadcasted_iota(jnp.int32, (chunk, lanes), 0)
        ahead = key_in_chunk - row_in_span

        def raw_scores(i, largest):
            found = dot(k_pos[key_place(i), :], q_rows[...], NT)
            found = jnp.where(ahead <= span * span_rows - first - i * chunk, found, -1e30)
            scores[score_place(i), :] = found
            return jnp.maximum(largest, jnp.max(found.reshape(chunk // 8, 8, lanes), axis=0))

        largest = lax.fori_loop(0, chunks, raw_scores, jnp.full((8, lanes), -1e30, jnp.float32))
        largest = jnp.max(largest, axis=0, keepdims=True)

        def weigh(i, total_weight):
            weight = jnp.exp2((scores[score_place(i), :] - largest) * (scaling * log2e))
            scores[score_place(i), :] = weight
            return total_weight + jnp.sum(weight.reshape(chunk // 8, 8, lanes), axis=0)

        weight_sum = lax.fori_loop(0, chunks, weigh, jnp.zeros((8, lanes), jnp.float32))
        inverse = 1.0 / jnp.sum(weight_sum, axis=0, keepdims=True)
        delta = delta_ref[local]

        query_grad[...] = jnp.zeros_like(query_grad)

        def gradients(i, carry):
            attention = scores[score_place(i), :] * inverse
            attention_grad = dot(v_pos[key_place(i), :], do_rows[...], NT)
            score_grad = (attention * (attention_grad - delta)).astype(jnp.bfloat16)
            keys = k_pos[key_place(i), :]
            grads[key_place(i), :head] += dot(score_grad, q_rows[...], NN)
            grads[key_place(i), head:] += dot(attention.astype(jnp.bfloat16), do_rows[...], NN)
            query_grad[...] += dot(keys, score_grad, TN)
            return carry

        lax.fori_loop(0, chunks, gradients, 0)
        turned = (query_grad[...] * scaling).T.astype(dq_ref.dtype)
        for h in range(heads):
            dq_ref[local * span_rows : (local + 1) * span_rows, h * head : (h + 1) * head] = turned[
                h * span_rows : (h + 1) * span_rows, :
            ]

    for piece, rows, place in spans_of_pieces():
        dkv_refs[piece][rows, :head] = (grads[place, :head] * scaling).astype(jnp.bfloat16)
        dkv_refs[piece][rows, head:] = grads[place, head:].astype(jnp.bfloat16)


def attention_grads(me, slots, docs, queries, grad_out, delta, key_values, head, block_tokens):
    rows, width = queries.shape
    low = len(key_values)
    total = low * key_values[0].shape[0]
    heads = width // head
    span_rows = rows // 2
    chunk = min(256, total)
    vmem = pl.BlockSpec(memory_space=pltpu.VMEM)
    smem = pl.BlockSpec(memory_space=pltpu.SMEM)
    lanes = heads * span_rows
    body = functools.partial(
        attention_kernel, low=low, span_rows=span_rows, block_tokens=block_tokens, chunk=chunk, heads=heads, head=head
    )
    return pl.pallas_call(
        body,
        out_shape=(
            jax.ShapeDtypeStruct((rows, width), jnp.bfloat16),
            *(jax.ShapeDtypeStruct((total // low, 2 * head), jnp.bfloat16) for _ in range(low)),
        ),
        in_specs=[smem, smem, smem, vmem, vmem, vmem] + [vmem] * low,
        out_specs=(vmem,) * (low + 1),
        scratch_shapes=[
            pltpu.VMEM((total + chunk, head), jnp.bfloat16),
            pltpu.VMEM((total + chunk, head), jnp.bfloat16),
            pltpu.VMEM((lanes, head), jnp.bfloat16),
            pltpu.VMEM((lanes, head), jnp.bfloat16),
            pltpu.VMEM((total + chunk, lanes), jnp.float32),
            pltpu.VMEM((total + chunk, 2 * head), jnp.float32),
            pltpu.VMEM((head, lanes), jnp.float32),
        ],
        compiler_params=pltpu.CompilerParams(vmem_limit_bytes=48 << 20),
        cost_estimate=pl.CostEstimate(flops=60000000000, transcendentals=0, bytes_accessed=0),
        name="attention_grads",
    )(me, slots, docs, queries, grad_out, delta, *key_values)


def weight_kernel(place, *refs, low, parts, splits, digits, last, head):
    grad_refs, refs = refs[: len(digits)], refs[len(digits) :]
    column_refs, refs = refs[: len(digits) * parts * len(splits)], refs[len(digits) * parts * len(splits) :]
    own_high, own_part = place[0] // low, place[1]
    high = column_refs[0].shape[0]
    rows = sum(splits)
    tokens = jnp.concatenate([ref[...].reshape(-1, ref.shape[-1]) for ref in column_refs], axis=0)
    grads = []
    for ref in grad_refs:
        for part in range(parts):
            for number, size in enumerate(splits):
                for h in range(high):
                    start = ((h ^ own_high) * parts + (part ^ own_part)) * rows + sum(splits[:number])
                    grads.append(ref[pl.ds(pl.multiple_of(start, 16), size), :])
    found = dot(jnp.concatenate(grads, axis=0), tokens, TN)
    if digits[0]:
        found = refs[0][...] + found
    if last:
        refs[-2][...] = found[:head, :].T
        refs[-1][...] = found[head:, :].T
    else:
        refs[-1][...] = found


def weight_step(place, digits, low, columns, grads, sums, head):
    count, _, width = columns[0][0].shape
    parts = len(columns)
    splits = [c.shape[1] for c in columns[0]]
    last = digits[-1] == low - 1
    columns = [c.reshape(count // low, low, c.shape[1], width) for part in columns for c in part]

    def spec(array, digit):
        return pl.BlockSpec(
            (count // low, 1, *array.shape[2:]), lambda i, place: (0, (place[0] % low) ^ digit, 0, 0)
        )

    shapes = ((width, head),) * 2 if last else ((2 * head, width),)
    before = [sums] if digits[0] else []
    return pl.pallas_call(
        functools.partial(
            weight_kernel, low=low, parts=parts, splits=splits, digits=digits, last=last, head=head
        ),
        out_shape=tuple(jax.ShapeDtypeStruct(s, jnp.float32) for s in shapes),
        grid_spec=pltpu.PrefetchScalarGridSpec(
            num_scalar_prefetch=1,
            grid=(1,),
            in_specs=[pl.BlockSpec(grads[d].shape, lambda i, place: (0, 0)) for d in digits]
            + [spec(c, d) for d in digits for c in columns]
            + [pl.BlockSpec((2 * head, width), lambda i, place: (0, 0))] * len(before),
            out_specs=tuple(pl.BlockSpec(s, lambda i, place: (0, 0)) for s in shapes),
        ),
        compiler_params=pltpu.CompilerParams(vmem_limit_bytes=32 << 20),
        name="weight_step",
    )(place, *(grads[d] for d in digits), *(columns * len(digits)), *before)


def after(value, *others):
    return lax.optimization_barrier((value, *others))[0]


def on_device(queries, keys, values, outputs, grad_out, inputs, block_doc, span_slots):
    batch_count, row_count, query_width = queries.shape
    head = keys.shape[2]
    heads = query_width // head
    span_rows = row_count // 2
    total = span_rows * span_slots.shape[0]
    block_tokens = total // block_doc.shape[1]
    count = total // row_count
    low = min(LOW, count)
    high = count // low
    token_rows = inputs.shape[1]
    tensor_count = row_count // token_rows
    column_count = inputs.shape[2] // count
    me = lax.axis_index("context").astype(jnp.int32).reshape(1)

    own = jnp.pad(keys, ((0, 0), (0, 0), (0, head))) + jnp.pad(values, ((0, 0), (0, 0), (head, 0)))
    by_high = [own] + [swap(own, k * low, count) for k in range(1, high)]
    column = jnp.concatenate(by_high, axis=1)

    sent = jnp.moveaxis(inputs.reshape(-1, count, column_count), 1, 0)
    column, sent = lax.optimization_barrier((column, sent))
    mine = [lax.all_to_all(sent, "context", split_axis=0, concat_axis=0, tiled=True)]

    key_values = [column] + [swap(column, k, count) for k in range(1, low)]
    delta = jnp.einsum(
        "bqgd,bqgd->bgq",
        grad_out.reshape(batch_count, row_count, heads, head),
        outputs.reshape(batch_count, row_count, heads, head),
        preferred_element_type=jnp.float32,
    )
    delta = delta.reshape(batch_count, heads, 2, span_rows).swapaxes(1, 2).reshape(batch_count, 2, 1, heads * span_rows)

    place = jnp.concatenate([me, lax.axis_index("tensor").astype(jnp.int32).reshape(1)])
    query_grads, key_sums, value_sums = [], 0.0, 0.0
    for b in range(batch_count):
        query_grad, *partials = attention_grads(
            me, span_slots, block_doc[b], queries[b], grad_out[b], delta[b], [kv[b] for kv in key_values], head, block_tokens
        )
        query_grads.append(query_grad)
        arrived = [partials[0]] + [swap(partials[k], k, count) for k in range(1, low)]
        sums = sum(p.astype(jnp.float32) for p in arrived)
        pieces = [sums[k * row_count : (k + 1) * row_count] for k in range(high)]
        arrived = [pieces[0]] + [swap(pieces[k].astype(jnp.bfloat16), k * low, count) for k in range(1, high)]
        own_grads = sum(p.astype(jnp.float32) for p in arrived).astype(jnp.bfloat16)
        column = jnp.concatenate([own_grads] + [swap(own_grads, k * low, count) for k in range(1, high)], axis=0)
        columns = [column] + [swap(column, k, count) for k in range(1, low)]
        held = [
            after(m.reshape(count, batch_count, -1, column_count)[:, b], w) for m, w in zip(mine, [own_grads])
        ]
        held = [held] + [
            [lax.ppermute(m, "tensor", [(i, i ^ k) for i in range(tensor_count)]) for m in held]
            for k in range(1, tensor_count)
        ]
        found = [None]
        for digits in [[0], [1], list(range(2, low))]:
            found = weight_step(place, digits, low, held, columns, found[0], head)
        key_sums, value_sums = key_sums + found[0], value_sums + found[1]
    return jnp.stack(query_grads), lax.psum(key_sums, "dp"), lax.psum(value_sums, "dp")


def solution(mesh):
    in_specs = (
        P("dp", "context", "tensor"),
        P("dp", "context", "tensor"),
        P("dp", "context", "tensor"),
        P("dp", "context", "tensor"),
        P("dp", "context", "tensor"),
        P("dp", ("context", "tensor"), None),
        P("dp", None),
        P(),
    )
    out_specs = (P("dp", "context", "tensor"), P("context", "tensor"), P("context", "tensor"))
    return jax.shard_map(on_device, mesh=mesh, in_specs=in_specs, out_specs=out_specs, check_vma=False)
```

```python
import functools
import math

import jax
import jax.numpy as jnp
from jax import lax
from jax.experimental import pallas as pl
from jax.experimental.pallas import tpu as pltpu
from jax.sharding import PartitionSpec as P

NT = (((1,), (1,)), ((), ()))
NN = (((1,), (0,)), ((), ()))
TN = (((0,), (0,)), ((), ()))

LOW = 4


def dot(left, right, dims):
    return lax.dot_general(left, right, dims, preferred_element_type=jnp.float32)


def swap(value, offset, count):
    return lax.ppermute(value, "context", [(i, i ^ offset) for i in range(count)])


def attention_kernel(
    me, slots, docs, q_ref, do_ref, delta_ref, *refs, low, span_rows, block_tokens, chunk, heads, head,
):
    kv_refs, (dq_ref, *dkv_refs), scratch = refs[:low], refs[low : 2 * low + 1], refs[2 * low + 1 :]
    k_pos, v_pos, q_rows, do_rows, scores, grads, query_grad = scratch
    slot_count = slots.shape[0]
    block_count = docs.shape[0]
    total = span_rows * slot_count
    lanes = heads * span_rows
    scaling = 1.0 / math.sqrt(head)
    log2e = 1.4426950408889634
    own = me[0]

    def spans_of_pieces():
        for r in range(slot_count // 2):
            for half in range(2):
                span = slots[2 * (own ^ r) + half]
                place = pl.ds(pl.multiple_of(span * span_rows, span_rows), span_rows)
                yield r % low, pl.ds((2 * (r // low) + half) * span_rows, span_rows), place

    for piece, rows, place in spans_of_pieces():
        k_pos[place, :] = kv_refs[piece][rows, :head]
        v_pos[place, :] = kv_refs[piece][rows, head:]
    k_pos[total:, :] = jnp.zeros((chunk, head), k_pos.dtype)
    v_pos[total:, :] = jnp.zeros((chunk, head), v_pos.dtype)
    grads[...] = jnp.zeros_like(grads)

    for local in range(2):
        span = slots[2 * own + local]
        document = docs[span * span_rows // block_tokens]
        first_block = lax.fori_loop(
            0, block_count, lambda b, n: n + (docs[b] < document).astype(jnp.int32), jnp.int32(0)
        )
        first = first_block * block_tokens
        chunks = ((span + 1) * span_rows - first + chunk - 1) // chunk
        for h in range(heads):
            source = (slice(local * span_rows, (local + 1) * span_rows), slice(h * head, (h + 1) * head))
            q_rows[h * span_rows : (h + 1) * span_rows, :] = q_ref[source]
            do_rows[h * span_rows : (h + 1) * span_rows, :] = do_ref[source]

        def key_place(i):
            return pl.ds(pl.multiple_of(first + i * chunk, span_rows), chunk)

        def score_place(i):
            return pl.ds(pl.multiple_of(i * chunk, chunk), chunk)

        row_in_span = lax.broadcasted_iota(jnp.int32, (chunk, lanes), 1) % span_rows
        key_in_chunk = lax.broadcasted_iota(jnp.int32, (chunk, lanes), 0)
        ahead = key_in_chunk - row_in_span

        def raw_scores(i, largest):
            found = dot(k_pos[key_place(i), :], q_rows[...], NT)
            found = jnp.where(ahead <= span * span_rows - first - i * chunk, found, -1e30)
            scores[score_place(i), :] = found
            return jnp.maximum(largest, jnp.max(found.reshape(chunk // 8, 8, lanes), axis=0))

        largest = lax.fori_loop(0, chunks, raw_scores, jnp.full((8, lanes), -1e30, jnp.float32))
        largest = jnp.max(largest, axis=0, keepdims=True)

        def weigh(i, total_weight):
            weight = jnp.exp2((scores[score_place(i), :] - largest) * (scaling * log2e))
            scores[score_place(i), :] = weight
            return total_weight + jnp.sum(weight.reshape(chunk // 8, 8, lanes), axis=0)

        weight_sum = lax.fori_loop(0, chunks, weigh, jnp.zeros((8, lanes), jnp.float32))
        inverse = 1.0 / jnp.sum(weight_sum, axis=0, keepdims=True)
        delta = delta_ref[local]

        query_grad[...] = jnp.zeros_like(query_grad)

        def gradients(i, carry):
            attention = scores[score_place(i), :] * inverse
            attention_grad = dot(v_pos[key_place(i), :], do_rows[...], NT)
            score_grad = (attention * (attention_grad - delta)).astype(jnp.bfloat16)
            keys = k_pos[key_place(i), :]
            grads[key_place(i), :head] += dot(score_grad, q_rows[...], NN)
            grads[key_place(i), head:] += dot(attention.astype(jnp.bfloat16), do_rows[...], NN)
            query_grad[...] += dot(keys, score_grad, TN)
            return carry

        lax.fori_loop(0, chunks, gradients, 0)
        turned = (query_grad[...] * scaling).T.astype(dq_ref.dtype)
        for h in range(heads):
            dq_ref[local * span_rows : (local + 1) * span_rows, h * head : (h + 1) * head] = turned[
                h * span_rows : (h + 1) * span_rows, :
            ]

    for piece, rows, place in spans_of_pieces():
        dkv_refs[piece][rows, :head] = (grads[place, :head] * scaling).astype(jnp.bfloat16)
        dkv_refs[piece][rows, head:] = grads[place, head:].astype(jnp.bfloat16)


def attention_grads(me, slots, docs, queries, grad_out, delta, key_values, head, block_tokens):
    rows, width = queries.shape
    low = len(key_values)
    total = low * key_values[0].shape[0]
    heads = width // head
    span_rows = rows // 2
    chunk = min(128, total)
    vmem = pl.BlockSpec(memory_space=pltpu.VMEM)
    smem = pl.BlockSpec(memory_space=pltpu.SMEM)
    lanes = heads * span_rows
    body = functools.partial(
        attention_kernel, low=low, span_rows=span_rows, block_tokens=block_tokens, chunk=chunk, heads=heads, head=head
    )
    return pl.pallas_call(
        body,
        out_shape=(
            jax.ShapeDtypeStruct((rows, width), jnp.bfloat16),
            *(jax.ShapeDtypeStruct((total // low, 2 * head), jnp.bfloat16) for _ in range(low)),
        ),
        in_specs=[smem, smem, smem, vmem, vmem, vmem] + [vmem] * low,
        out_specs=(vmem,) * (low + 1),
        scratch_shapes=[
            pltpu.VMEM((total + chunk, head), jnp.bfloat16),
            pltpu.VMEM((total + chunk, head), jnp.bfloat16),
            pltpu.VMEM((lanes, head), jnp.bfloat16),
            pltpu.VMEM((lanes, head), jnp.bfloat16),
            pltpu.VMEM((total + chunk, lanes), jnp.float32),
            pltpu.VMEM((total + chunk, 2 * head), jnp.float32),
            pltpu.VMEM((head, lanes), jnp.float32),
        ],
        compiler_params=pltpu.CompilerParams(vmem_limit_bytes=48 << 20),
        cost_estimate=pl.CostEstimate(flops=60000000000, transcendentals=0, bytes_accessed=0),
        name="attention_grads",
    )(me, slots, docs, queries, grad_out, delta, *key_values)


def weight_kernel(place, *refs, low, parts, digits, more, last, head):
    grad_refs, refs = refs[: len(digits)], refs[len(digits) :]
    column_refs, refs = refs[:parts], refs[parts:]
    own_high, own_low, own_part = place[0] // low, place[0] % low, place[1]
    high, _, rows, width = column_refs[0].shape
    tokens, grads = [], []
    for digit, grad_ref in zip(digits, grad_refs):
        for part, ref in enumerate(column_refs):
            for h in range(high):
                tokens.append(ref[h, own_low ^ digit])
                start = ((h ^ own_high) * parts + (part ^ own_part)) * rows
                grads.append(grad_ref[pl.ds(pl.multiple_of(start, rows), rows), :])
    found = dot(jnp.concatenate(grads, axis=0), jnp.concatenate(tokens, axis=0), TN)
    if more:
        found = refs[0][...] + found
    if last:
        refs[-2][...] = found[:head, :].T
        refs[-1][...] = found[head:, :].T
    else:
        refs[-1][...] = found


def weight_step(place, digits, low, columns, grads, sums, head):
    count, rows, width = columns[0].shape
    parts = len(columns)
    last = digits[-1] == low - 1
    columns = [c.reshape(count // low, low, rows, width) for c in columns]
    shapes = ((width, head),) * 2 if last else ((2 * head, width),)
    operands = [grads[d] for d in digits] + columns + ([] if sums is None else [sums])
    vmem = pl.BlockSpec(memory_space=pltpu.VMEM)
    return pl.pallas_call(
        functools.partial(
            weight_kernel, low=low, parts=parts, digits=digits, more=sums is not None, last=last, head=head
        ),
        out_shape=tuple(jax.ShapeDtypeStruct(s, jnp.float32) for s in shapes),
        in_specs=[pl.BlockSpec(memory_space=pltpu.SMEM)] + [vmem] * len(operands),
        out_specs=(vmem,) * len(shapes),
        compiler_params=pltpu.CompilerParams(vmem_limit_bytes=24 << 20),
        name="weight_step",
    )(place, *operands)


def after(value, *others):
    return lax.optimization_barrier((value, *others))[0]


def on_device(queries, keys, values, outputs, grad_out, inputs, block_doc, span_slots):
    batch_count, row_count, query_width = queries.shape
    head = keys.shape[2]
    heads = query_width // head
    span_rows = row_count // 2
    total = span_rows * span_slots.shape[0]
    block_tokens = total // block_doc.shape[1]
    count = total // row_count
    low = min(LOW, count)
    high = count // low
    token_rows = inputs.shape[1]
    tensor_count = row_count // token_rows
    column_count = inputs.shape[2] // count
    me = lax.axis_index("context").astype(jnp.int32).reshape(1)

    own = jnp.pad(keys, ((0, 0), (0, 0), (0, head))) + jnp.pad(values, ((0, 0), (0, 0), (head, 0)))
    by_high = [own] + [swap(own, k * low, count) for k in range(1, high)]
    column = jnp.concatenate(by_high, axis=1)

    sent = jnp.moveaxis(inputs.reshape(-1, count, column_count), 1, 0)
    column, sent = lax.optimization_barrier((column, sent))
    mine = lax.all_to_all(sent, "context", split_axis=0, concat_axis=0, tiled=True)

    key_values = [column] + [swap(column, k, count) for k in range(1, low)]
    delta = jnp.einsum(
        "bqgd,bqgd->bgq",
        grad_out.reshape(batch_count, row_count, heads, head),
        outputs.reshape(batch_count, row_count, heads, head),
        preferred_element_type=jnp.float32,
    )
    delta = delta.reshape(batch_count, heads, 2, span_rows).swapaxes(1, 2).reshape(batch_count, 2, 1, heads * span_rows)

    place = jnp.concatenate([me, lax.axis_index("tensor").astype(jnp.int32).reshape(1)])
    query_grads, key_sums, value_sums = [], 0.0, 0.0
    for b in range(batch_count):
        query_grad, *partials = attention_grads(
            me, span_slots, block_doc[b], queries[b], grad_out[b], delta[b], [kv[b] for kv in key_values], head, block_tokens
        )
        query_grads.append(query_grad)
        arrived = [partials[0]] + [swap(partials[k], k, count) for k in range(1, low)]
        sums = sum(p.astype(jnp.float32) for p in arrived)
        pieces = [sums[k * row_count : (k + 1) * row_count] for k in range(high)]
        arrived = [pieces[0]] + [swap(pieces[k].astype(jnp.bfloat16), k * low, count) for k in range(1, high)]
        own_grads = sum(p.astype(jnp.float32) for p in arrived).astype(jnp.bfloat16)
        column = jnp.concatenate([own_grads] + [swap(own_grads, k * low, count) for k in range(1, high)], axis=0)
        columns = [column] + [swap(column, k, count) for k in range(1, low)]
        held = after(mine.reshape(count, batch_count, -1, column_count)[:, b], own_grads)
        held = [held] + [
            lax.ppermute(held, "tensor", [(i, i ^ k) for i in range(tensor_count)]) for k in range(1, tensor_count)
        ]
        found = [None]
        for digits in [[0], [1], list(range(2, low))]:
            found = weight_step(place, digits, low, held, columns, found[0], head)
        key_sums, value_sums = key_sums + found[0], value_sums + found[1]
    return jnp.stack(query_grads), lax.psum(key_sums, "dp"), lax.psum(value_sums, "dp")


def solution(mesh):
    in_specs = (
        P("dp", "context", "tensor"),
        P("dp", "context", "tensor"),
        P("dp", "context", "tensor"),
        P("dp", "context", "tensor"),
        P("dp", "context", "tensor"),
        P("dp", ("context", "tensor"), None),
        P("dp", None),
        P(),
    )
    out_specs = (P("dp", "context", "tensor"), P("context", "tensor"), P("context", "tensor"))
    return jax.shard_map(on_device, mesh=mesh, in_specs=in_specs, out_specs=out_specs, check_vma=False)
```

```python
import functools
import math

import jax
import jax.numpy as jnp
from jax import lax
from jax.experimental import pallas as pl
from jax.experimental.pallas import tpu as pltpu
from jax.sharding import PartitionSpec as P

NT = (((1,), (1,)), ((), ()))
NN = (((1,), (0,)), ((), ()))
TN = (((0,), (0,)), ((), ()))

LOW = 4


def dot(left, right, dims):
    return lax.dot_general(left, right, dims, preferred_element_type=jnp.float32)


def swap(value, offset, count):
    return lax.ppermute(value, "context", [(i, i ^ offset) for i in range(count)])


def attention_kernel(
    me, slots, docs, q_ref, do_ref, delta_ref, *refs, low, span_rows, block_tokens, chunk, heads, head,
):
    kv_refs, (dq_ref, *dkv_refs), scratch = refs[:low], refs[low : 2 * low + 1], refs[2 * low + 1 :]
    k_pos, v_pos, q_rows, do_rows, scores, grads, query_grad = scratch
    slot_count = slots.shape[0]
    block_count = docs.shape[0]
    total = span_rows * slot_count
    lanes = heads * span_rows
    scaling = 1.0 / math.sqrt(head)
    log2e = 1.4426950408889634
    own = me[0]

    def spans_of_pieces():
        for r in range(slot_count // 2):
            for half in range(2):
                span = slots[2 * (own ^ r) + half]
                place = pl.ds(pl.multiple_of(span * span_rows, span_rows), span_rows)
                yield r % low, pl.ds((2 * (r // low) + half) * span_rows, span_rows), place

    for piece, rows, place in spans_of_pieces():
        k_pos[place, :] = kv_refs[piece][rows, :head]
        v_pos[place, :] = kv_refs[piece][rows, head:]
    k_pos[total:, :] = jnp.zeros((chunk, head), k_pos.dtype)
    v_pos[total:, :] = jnp.zeros((chunk, head), v_pos.dtype)
    grads[...] = jnp.zeros_like(grads)

    for local in range(2):
        span = slots[2 * own + local]
        document = docs[span * span_rows // block_tokens]
        first_block = lax.fori_loop(
            0, block_count, lambda b, n: n + (docs[b] < document).astype(jnp.int32), jnp.int32(0)
        )
        first = first_block * block_tokens
        chunks = ((span + 1) * span_rows - first + chunk - 1) // chunk
        for h in range(heads):
            source = (slice(local * span_rows, (local + 1) * span_rows), slice(h * head, (h + 1) * head))
            q_rows[h * span_rows : (h + 1) * span_rows, :] = q_ref[source]
            do_rows[h * span_rows : (h + 1) * span_rows, :] = do_ref[source]

        def key_place(i):
            return pl.ds(pl.multiple_of(first + i * chunk, span_rows), chunk)

        def score_place(i):
            return pl.ds(pl.multiple_of(i * chunk, chunk), chunk)

        def raw_scores(i, largest, masked):
            found = dot(k_pos[key_place(i), :], q_rows[...], NT)
            if masked:
                row_in_span = lax.broadcasted_iota(jnp.int32, (chunk, lanes), 1) % span_rows
                ahead = lax.broadcasted_iota(jnp.int32, (chunk, lanes), 0) - row_in_span
                found = jnp.where(ahead <= span * span_rows - first - i * chunk, found, -1e30)
            scores[score_place(i), :] = found
            return jnp.maximum(largest, jnp.max(found.reshape(chunk // 8, 8, lanes), axis=0))

        largest = lax.fori_loop(
            0, chunks - 1, functools.partial(raw_scores, masked=False), jnp.full((8, lanes), -1e30, jnp.float32)
        )
        largest = raw_scores(chunks - 1, largest, True)
        largest = jnp.max(largest, axis=0, keepdims=True)

        def weigh(i, total_weight):
            weight = jnp.exp2((scores[score_place(i), :] - largest) * (scaling * log2e))
            scores[score_place(i), :] = weight
            return total_weight + jnp.sum(weight.reshape(chunk // 8, 8, lanes), axis=0)

        weight_sum = lax.fori_loop(0, chunks, weigh, jnp.zeros((8, lanes), jnp.float32))
        inverse = 1.0 / jnp.sum(weight_sum, axis=0, keepdims=True)
        delta = delta_ref[local]

        query_grad[...] = jnp.zeros_like(query_grad)

        def gradients(i, carry):
            attention = scores[score_place(i), :] * inverse
            attention_grad = dot(v_pos[key_place(i), :], do_rows[...], NT)
            score_grad = (attention * (attention_grad - delta)).astype(jnp.bfloat16)
            keys = k_pos[key_place(i), :]
            grads[key_place(i), :head] += dot(score_grad, q_rows[...], NN)
            grads[key_place(i), head:] += dot(attention.astype(jnp.bfloat16), do_rows[...], NN)
            query_grad[...] += dot(keys, score_grad, TN)
            return carry

        lax.fori_loop(0, chunks, gradients, 0)
        turned = (query_grad[...] * scaling).T.astype(dq_ref.dtype)
        for h in range(heads):
            dq_ref[local * span_rows : (local + 1) * span_rows, h * head : (h + 1) * head] = turned[
                h * span_rows : (h + 1) * span_rows, :
            ]

    for piece, rows, place in spans_of_pieces():
        dkv_refs[piece][rows, :head] = (grads[place, :head] * scaling).astype(jnp.bfloat16)
        dkv_refs[piece][rows, head:] = grads[place, head:].astype(jnp.bfloat16)


def attention_grads(me, slots, docs, queries, grad_out, delta, key_values, head, block_tokens):
    rows, width = queries.shape
    low = len(key_values)
    total = low * key_values[0].shape[0]
    heads = width // head
    span_rows = rows // 2
    chunk = min(128, total)
    vmem = pl.BlockSpec(memory_space=pltpu.VMEM)
    smem = pl.BlockSpec(memory_space=pltpu.SMEM)
    lanes = heads * span_rows
    body = functools.partial(
        attention_kernel, low=low, span_rows=span_rows, block_tokens=block_tokens, chunk=chunk, heads=heads, head=head
    )
    return pl.pallas_call(
        body,
        out_shape=(
            jax.ShapeDtypeStruct((rows, width), jnp.bfloat16),
            *(jax.ShapeDtypeStruct((total // low, 2 * head), jnp.bfloat16) for _ in range(low)),
        ),
        in_specs=[smem, smem, smem, vmem, vmem, vmem] + [vmem] * low,
        out_specs=(vmem,) * (low + 1),
        scratch_shapes=[
            pltpu.VMEM((total + chunk, head), jnp.bfloat16),
            pltpu.VMEM((total + chunk, head), jnp.bfloat16),
            pltpu.VMEM((lanes, head), jnp.bfloat16),
            pltpu.VMEM((lanes, head), jnp.bfloat16),
            pltpu.VMEM((total + chunk, lanes), jnp.float32),
            pltpu.VMEM((total + chunk, 2 * head), jnp.float32),
            pltpu.VMEM((head, lanes), jnp.float32),
        ],
        compiler_params=pltpu.CompilerParams(vmem_limit_bytes=48 << 20),
        cost_estimate=pl.CostEstimate(flops=60000000000, transcendentals=0, bytes_accessed=0),
        name="attention_grads",
    )(me, slots, docs, queries, grad_out, delta, *key_values)


def weight_kernel(place, *refs, low, parts, digits, more, last, head):
    grad_refs, refs = refs[: len(digits)], refs[len(digits) :]
    column_refs, refs = refs[:parts], refs[parts:]
    own_high, own_low, own_part = place[0] // low, place[0] % low, place[1]
    high, _, rows, width = column_refs[0].shape
    tokens, grads = [], []
    for digit, grad_ref in zip(digits, grad_refs):
        for part, ref in enumerate(column_refs):
            for h in range(high):
                tokens.append(ref[h, own_low ^ digit])
                start = ((h ^ own_high) * parts + (part ^ own_part)) * rows
                grads.append(grad_ref[pl.ds(pl.multiple_of(start, rows), rows), :])
    found = dot(jnp.concatenate(tokens, axis=0), jnp.concatenate(grads, axis=0), TN)
    if more:
        found = refs[0][...] + found
    if last:
        refs[-2][...] = found[:, :head]
        refs[-1][...] = found[:, head:]
    else:
        refs[-1][...] = found


def weight_step(place, digits, low, columns, grads, sums, head):
    count, rows, width = columns[0].shape
    parts = len(columns)
    last = digits[-1] == low - 1
    columns = [c.reshape(count // low, low, rows, width) for c in columns]
    shapes = ((width, head),) * 2 if last else ((width, 2 * head),)
    operands = [grads[d] for d in digits] + columns + ([] if sums is None else [sums])
    vmem = pl.BlockSpec(memory_space=pltpu.VMEM)
    return pl.pallas_call(
        functools.partial(
            weight_kernel, low=low, parts=parts, digits=digits, more=sums is not None, last=last, head=head
        ),
        out_shape=tuple(jax.ShapeDtypeStruct(s, jnp.float32) for s in shapes),
        in_specs=[pl.BlockSpec(memory_space=pltpu.SMEM)] + [vmem] * len(operands),
        out_specs=(vmem,) * len(shapes),
        compiler_params=pltpu.CompilerParams(vmem_limit_bytes=24 << 20),
        name="weight_step",
    )(place, *operands)


def after(value, *others):
    return lax.optimization_barrier((value, *others))[0]


def on_device(queries, keys, values, outputs, grad_out, inputs, block_doc, span_slots):
    batch_count, row_count, query_width = queries.shape
    head = keys.shape[2]
    heads = query_width // head
    span_rows = row_count // 2
    total = span_rows * span_slots.shape[0]
    block_tokens = total // block_doc.shape[1]
    count = total // row_count
    low = min(LOW, count)
    high = count // low
    token_rows = inputs.shape[1]
    tensor_count = row_count // token_rows
    column_count = inputs.shape[2] // count
    me = lax.axis_index("context").astype(jnp.int32).reshape(1)

    own = jnp.pad(keys, ((0, 0), (0, 0), (0, head))) + jnp.pad(values, ((0, 0), (0, 0), (head, 0)))
    by_high = [own] + [swap(own, k * low, count) for k in range(1, high)]
    column = jnp.concatenate(by_high, axis=1)

    sent = jnp.moveaxis(inputs.reshape(-1, count, column_count), 1, 0)
    column, sent = lax.optimization_barrier((column, sent))
    mine = lax.all_to_all(sent, "context", split_axis=0, concat_axis=0, tiled=True)

    key_values = [column] + [swap(column, k, count) for k in range(1, low)]
    delta = jnp.einsum(
        "bqgd,bqgd->bgq",
        grad_out.reshape(batch_count, row_count, heads, head),
        outputs.reshape(batch_count, row_count, heads, head),
        preferred_element_type=jnp.float32,
    )
    delta = delta.reshape(batch_count, heads, 2, span_rows).swapaxes(1, 2).reshape(batch_count, 2, 1, heads * span_rows)

    place = jnp.concatenate([me, lax.axis_index("tensor").astype(jnp.int32).reshape(1)])
    query_grads, key_sums, value_sums = [], 0.0, 0.0
    for b in range(batch_count):
        query_grad, *partials = attention_grads(
            me, span_slots, block_doc[b], queries[b], grad_out[b], delta[b], [kv[b] for kv in key_values], head, block_tokens
        )
        query_grads.append(query_grad)
        arrived = [partials[0]] + [swap(partials[k], k, count) for k in range(1, low)]
        sums = sum(p.astype(jnp.float32) for p in arrived)
        pieces = [sums[k * row_count : (k + 1) * row_count] for k in range(high)]
        arrived = [pieces[0]] + [swap(pieces[k].astype(jnp.bfloat16), k * low, count) for k in range(1, high)]
        own_grads = sum(p.astype(jnp.float32) for p in arrived).astype(jnp.bfloat16)
        column = jnp.concatenate([own_grads] + [swap(own_grads, k * low, count) for k in range(1, high)], axis=0)
        columns = [column] + [swap(column, k, count) for k in range(1, low)]
        held = after(mine.reshape(count, batch_count, -1, column_count)[:, b], column)
        held = [held] + [
            lax.ppermute(held, "tensor", [(i, i ^ k) for i in range(tensor_count)]) for k in range(1, tensor_count)
        ]
        found = [None]
        for digits in [[0], [1], list(range(2, low))]:
            found = weight_step(place, digits, low, held, columns, found[0], head)
        key_sums, value_sums = key_sums + found[0], value_sums + found[1]
    return jnp.stack(query_grads), lax.psum(key_sums, "dp"), lax.psum(value_sums, "dp")


def solution(mesh):
    in_specs = (
        P("dp", "context", "tensor"),
        P("dp", "context", "tensor"),
        P("dp", "context", "tensor"),
        P("dp", "context", "tensor"),
        P("dp", "context", "tensor"),
        P("dp", ("context", "tensor"), None),
        P("dp", None),
        P(),
    )
    out_specs = (P("dp", "context", "tensor"), P("context", "tensor"), P("context", "tensor"))
    return jax.shard_map(on_device, mesh=mesh, in_specs=in_specs, out_specs=out_specs, check_vma=False)
```

```python
import functools
import math

import jax
import jax.numpy as jnp
from jax import lax
from jax.experimental import pallas as pl
from jax.experimental.pallas import tpu as pltpu
from jax.sharding import PartitionSpec as P

NT = (((1,), (1,)), ((), ()))
NN = (((1,), (0,)), ((), ()))
TN = (((0,), (0,)), ((), ()))

LOW = 4


def dot(left, right, dims):
    return lax.dot_general(left, right, dims, preferred_element_type=jnp.float32)


def swap(value, offset, count):
    return lax.ppermute(value, "context", [(i, i ^ offset) for i in range(count)])


def attention_kernel(
    me, slots, docs, q_ref, do_ref, delta_ref, *refs, low, span_rows, block_tokens, chunk, heads, head,
):
    kv_refs, (dq_ref, *dkv_refs), scratch = refs[:low], refs[low : 2 * low + 1], refs[2 * low + 1 :]
    k_pos, v_pos, q_rows, do_rows, scores, grads, query_grad = scratch
    slot_count = slots.shape[0]
    block_count = docs.shape[0]
    total = span_rows * slot_count
    lanes = heads * span_rows
    scaling = 1.0 / math.sqrt(head)
    log2e = 1.4426950408889634
    own = me[0]

    def spans_of_pieces():
        for r in range(slot_count // 2):
            for half in range(2):
                span = slots[2 * (own ^ r) + half]
                place = pl.ds(pl.multiple_of(span * span_rows, span_rows), span_rows)
                yield r % low, pl.ds((2 * (r // low) + half) * span_rows, span_rows), place

    for piece, rows, place in spans_of_pieces():
        k_pos[place, :] = kv_refs[piece][rows, :head]
        v_pos[place, :] = kv_refs[piece][rows, head:]
    k_pos[total:, :] = jnp.zeros((chunk, head), k_pos.dtype)
    v_pos[total:, :] = jnp.zeros((chunk, head), v_pos.dtype)
    grads[...] = jnp.zeros_like(grads)

    for local in range(2):
        span = slots[2 * own + local]
        document = docs[span * span_rows // block_tokens]
        first_block = lax.fori_loop(
            0, block_count, lambda b, n: n + (docs[b] < document).astype(jnp.int32), jnp.int32(0)
        )
        first = first_block * block_tokens
        chunks = ((span + 1) * span_rows - first + chunk - 1) // chunk
        for h in range(heads):
            source = (slice(local * span_rows, (local + 1) * span_rows), slice(h * head, (h + 1) * head))
            q_rows[h * span_rows : (h + 1) * span_rows, :] = q_ref[source]
            do_rows[h * span_rows : (h + 1) * span_rows, :] = do_ref[source]

        def key_place(i):
            return pl.ds(pl.multiple_of(first + i * chunk, span_rows), chunk)

        def score_place(i):
            return pl.ds(pl.multiple_of(i * chunk, chunk), chunk)

        row_in_span = lax.broadcasted_iota(jnp.int32, (chunk, lanes), 1) % span_rows
        key_in_chunk = lax.broadcasted_iota(jnp.int32, (chunk, lanes), 0)
        ahead = key_in_chunk - row_in_span

        def raw_scores(i, largest):
            found = dot(k_pos[key_place(i), :], q_rows[...], NT)
            found = jnp.where(ahead <= span * span_rows - first - i * chunk, found, -1e30)
            scores[score_place(i), :] = found
            return jnp.maximum(largest, jnp.max(found.reshape(chunk // 8, 8, lanes), axis=0))

        largest = lax.fori_loop(0, chunks, raw_scores, jnp.full((8, lanes), -1e30, jnp.float32))
        largest = jnp.max(largest, axis=0, keepdims=True)

        def weigh(i, total_weight):
            weight = jnp.exp2((scores[score_place(i), :] - largest) * (scaling * log2e))
            scores[score_place(i), :] = weight
            return total_weight + jnp.sum(weight.reshape(chunk // 8, 8, lanes), axis=0)

        weight_sum = lax.fori_loop(0, chunks, weigh, jnp.zeros((8, lanes), jnp.float32))
        inverse = 1.0 / jnp.sum(weight_sum, axis=0, keepdims=True)
        delta = delta_ref[local]

        query_grad[...] = jnp.zeros_like(query_grad)

        def gradients(i, carry):
            attention = scores[score_place(i), :] * inverse
            attention_grad = dot(v_pos[key_place(i), :], do_rows[...], NT)
            score_grad = (attention * (attention_grad - delta)).astype(jnp.bfloat16)
            keys = k_pos[key_place(i), :]
            grads[key_place(i), :head] += dot(score_grad, q_rows[...], NN)
            grads[key_place(i), head:] += dot(attention.astype(jnp.bfloat16), do_rows[...], NN)
            query_grad[...] += dot(keys, score_grad, TN)
            return carry

        lax.fori_loop(0, chunks, gradients, 0)
        turned = (query_grad[...] * scaling).T.astype(dq_ref.dtype)
        for h in range(heads):
            dq_ref[local * span_rows : (local + 1) * span_rows, h * head : (h + 1) * head] = turned[
                h * span_rows : (h + 1) * span_rows, :
            ]

    for piece, rows, place in spans_of_pieces():
        dkv_refs[piece][rows, :head] = (grads[place, :head] * scaling).astype(jnp.bfloat16)
        dkv_refs[piece][rows, head:] = grads[place, head:].astype(jnp.bfloat16)


def attention_grads(me, slots, docs, queries, grad_out, delta, key_values, head, block_tokens):
    rows, width = queries.shape
    low = len(key_values)
    total = low * key_values[0].shape[0]
    heads = width // head
    span_rows = rows // 2
    chunk = min(128, total)
    vmem = pl.BlockSpec(memory_space=pltpu.VMEM)
    smem = pl.BlockSpec(memory_space=pltpu.SMEM)
    lanes = heads * span_rows
    body = functools.partial(
        attention_kernel, low=low, span_rows=span_rows, block_tokens=block_tokens, chunk=chunk, heads=heads, head=head
    )
    return pl.pallas_call(
        body,
        out_shape=(
            jax.ShapeDtypeStruct((rows, width), jnp.bfloat16),
            *(jax.ShapeDtypeStruct((total // low, 2 * head), jnp.bfloat16) for _ in range(low)),
        ),
        in_specs=[smem, smem, smem, vmem, vmem, vmem] + [vmem] * low,
        out_specs=(vmem,) * (low + 1),
        scratch_shapes=[
            pltpu.VMEM((total + chunk, head), jnp.bfloat16),
            pltpu.VMEM((total + chunk, head), jnp.bfloat16),
            pltpu.VMEM((lanes, head), jnp.bfloat16),
            pltpu.VMEM((lanes, head), jnp.bfloat16),
            pltpu.VMEM((total + chunk, lanes), jnp.float32),
            pltpu.VMEM((total + chunk, 2 * head), jnp.float32),
            pltpu.VMEM((head, lanes), jnp.float32),
        ],
        compiler_params=pltpu.CompilerParams(vmem_limit_bytes=48 << 20),
        cost_estimate=pl.CostEstimate(flops=60000000000, transcendentals=0, bytes_accessed=0),
        name="attention_grads",
    )(me, slots, docs, queries, grad_out, delta, *key_values)


def weight_kernel(place, *refs, low, parts, digits, more, last, head):
    grad_refs, refs = refs[: len(digits)], refs[len(digits) :]
    column_refs, refs = refs[:parts], refs[parts:]
    own_high, own_low, own_part = place[0] // low, place[0] % low, place[1]
    high, _, rows, width = column_refs[0].shape
    tokens, grads = [], []
    for digit, grad_ref in zip(digits, grad_refs):
        for part, ref in enumerate(column_refs):
            for h in range(high):
                tokens.append(ref[h, own_low ^ digit])
                start = ((h ^ own_high) * parts + (part ^ own_part)) * rows
                grads.append(grad_ref[pl.ds(pl.multiple_of(start, rows), rows), :])
    found = dot(jnp.concatenate(grads, axis=0), jnp.concatenate(tokens, axis=0), TN)
    if more:
        found = refs[0][...] + found
    if last:
        refs[-2][...] = found[:head, :].T
        refs[-1][...] = found[head:, :].T
    else:
        refs[-1][...] = found


def weight_step(place, digits, low, columns, grads, sums, head):
    count, rows, width = columns[0].shape
    parts = len(columns)
    last = digits[-1] == low - 1
    columns = [c.reshape(count // low, low, rows, width) for c in columns]
    shapes = ((width, head),) * 2 if last else ((2 * head, width),)
    operands = [grads[d] for d in digits] + columns + ([] if sums is None else [sums])
    vmem = pl.BlockSpec(memory_space=pltpu.VMEM)
    return pl.pallas_call(
        functools.partial(
            weight_kernel, low=low, parts=parts, digits=digits, more=sums is not None, last=last, head=head
        ),
        out_shape=tuple(jax.ShapeDtypeStruct(s, jnp.float32) for s in shapes),
        in_specs=[pl.BlockSpec(memory_space=pltpu.SMEM)] + [vmem] * len(operands),
        out_specs=(vmem,) * len(shapes),
        compiler_params=pltpu.CompilerParams(vmem_limit_bytes=24 << 20),
        name="weight_step",
    )(place, *operands)


def after(value, *others):
    return lax.optimization_barrier((value, *others))[0]


def on_device(queries, keys, values, outputs, grad_out, inputs, block_doc, span_slots):
    batch_count, row_count, query_width = queries.shape
    head = keys.shape[2]
    heads = query_width // head
    span_rows = row_count // 2
    total = span_rows * span_slots.shape[0]
    block_tokens = total // block_doc.shape[1]
    count = total // row_count
    low = min(LOW, count)
    high = count // low
    token_rows = inputs.shape[1]
    tensor_count = row_count // token_rows
    column_count = inputs.shape[2] // count
    me = lax.axis_index("context").astype(jnp.int32).reshape(1)

    own = jnp.pad(keys, ((0, 0), (0, 0), (0, head))) + jnp.pad(values, ((0, 0), (0, 0), (head, 0)))
    by_high = [own] + [swap(own, k * low, count) for k in range(1, high)]
    column = jnp.concatenate(by_high, axis=1)

    sent = jnp.moveaxis(inputs.reshape(-1, count, column_count), 1, 0)
    column, sent = lax.optimization_barrier((column, sent))
    mine = lax.all_to_all(sent, "context", split_axis=0, concat_axis=0, tiled=True)

    key_values = [column] + [swap(column, k, count) for k in range(1, low)]
    delta = jnp.einsum(
        "bqgd,bqgd->bgq",
        grad_out.reshape(batch_count, row_count, heads, head),
        outputs.reshape(batch_count, row_count, heads, head),
        preferred_element_type=jnp.float32,
    )
    delta = delta.reshape(batch_count, heads, 2, span_rows).swapaxes(1, 2).reshape(batch_count, 2, 1, heads * span_rows)

    place = jnp.concatenate([me, lax.axis_index("tensor").astype(jnp.int32).reshape(1)])
    query_grads, key_sums, value_sums = [], 0.0, 0.0
    for b in range(batch_count):
        query_grad, *partials = attention_grads(
            me, span_slots, block_doc[b], queries[b], grad_out[b], delta[b], [kv[b] for kv in key_values], head, block_tokens
        )
        query_grads.append(query_grad)
        arrived = [partials[0]] + [swap(partials[k], k, count) for k in range(1, low)]
        sums = sum(p.astype(jnp.float32) for p in arrived)
        pieces = [sums[k * row_count : (k + 1) * row_count] for k in range(high)]
        arrived = [pieces[0]] + [swap(pieces[k].astype(jnp.bfloat16), k * low, count) for k in range(1, high)]
        own_grads = sum(p.astype(jnp.float32) for p in arrived).astype(jnp.bfloat16)
        column = jnp.concatenate([own_grads] + [swap(own_grads, k * low, count) for k in range(1, high)], axis=0)
        columns = [column] + [swap(column, k, count) for k in range(1, low)]
        held = after(mine.reshape(count, batch_count, -1, column_count)[:, b], column)
        held = [held] + [
            lax.ppermute(held, "tensor", [(i, i ^ k) for i in range(tensor_count)]) for k in range(1, tensor_count)
        ]
        found = [None]
        for digits in [[0], [1], list(range(2, low))]:
            found = weight_step(place, digits, low, held, columns, found[0], head)
        key_sums, value_sums = key_sums + found[0], value_sums + found[1]
    return jnp.stack(query_grads), lax.psum(key_sums, "dp"), lax.psum(value_sums, "dp")


def solution(mesh):
    in_specs = (
        P("dp", "context", "tensor"),
        P("dp", "context", "tensor"),
        P("dp", "context", "tensor"),
        P("dp", "context", "tensor"),
        P("dp", "context", "tensor"),
        P("dp", ("context", "tensor"), None),
        P("dp", None),
        P(),
    )
    out_specs = (P("dp", "context", "tensor"), P("context", "tensor"), P("context", "tensor"))
    return jax.shard_map(on_device, mesh=mesh, in_specs=in_specs, out_specs=out_specs, check_vma=False)
```
